256 devices in a mesh: row: 8 (over x, core), col: 16 (over y, z_hi), rep: 2 (over z_lo).
Axes of the slice: x: 4, y: 4, z: 8 (z_hi: 4, z_lo: 2; z = z_hi * 2 + z_lo), core: 2. Of those that a mesh axis runs over, the one named last changes fastest.
Arguments:
- slab_half: float32 [2, 8192, 4096], P('rep', 'row', 'col'), may hold values from -6 to 6
- window_half: float32 [2, 4096, 8192], P('rep', 'row', 'col'), may hold values from -0.125 to 0.125
- slab_cols: int32 [64, 20], replicated, may hold values from 0 to 63, as said below
- window_cols: int32 [64, 20], replicated, may hold values from 0 to 63, as said below
Outputs:
- slab_square: float32 [8192, 8192], P(('row', 'rep'), 'col')
The draws below stay inside these ranges and needn't reach their ends.
Inputs may be any that keep to these rules, and one draw needn't show every extreme that they name: `slab_cols`: each slab block row i lists 20 distinct block columns, all within 24 blocks of its centre, block column i; it lists the column exactly 24 blocks above the centre where that column exists, else the one exactly 24 blocks below where that exists. `window_cols`: each window block row k lists 20 distinct block columns, all within 24 blocks of column k; it lists column k + 24 where that column exists, else column k - 24 where that exists.
All inputs are finite; a program needn't handle non-finite values.
Results may differ from the reference program's by a relative error of at most 0.0001.
Values sent between devices are 32-bit elements; how exact they have to be, the bound alone decides.
A program may use at most 128 MiB of HBM per device.

```python
import jax
import jax.numpy as jnp
from jax import lax

BS = 128
KL = 20
BAND = 24
NI = 64
NK = 64
KH = 32
N_REP = 2


def banded_columns(key, centers):
    height = centers.shape[0]
    noise = jax.random.randint(key, (height, NK), 0, 65536, dtype=jnp.int32)
    columns = jnp.arange(NK, dtype=jnp.int32)
    distance = jnp.abs(columns[None, :] - centers[:, None])
    inside = distance <= BAND
    upper = centers + BAND
    lower_edge = centers - BAND
    edge = jnp.where(upper <= NK - 1, upper, lower_edge)
    forced = columns[None, :] == edge[:, None]
    score = jnp.where(inside, (noise + 1) * NK + columns[None, :], columns[None, :])
    score = jnp.where(forced, 131072 * NK + columns[None, :], score)
    chosen = lax.top_k(score, KL)[1]
    return chosen.astype(jnp.int32)


def draw_slab_cols(key, part):
    centers = jnp.arange(NI, dtype=jnp.int32) * NK // NI
    return banded_columns(jax.random.fold_in(key, 11), centers)


def draw_window_cols(key, part):
    return banded_columns(jax.random.fold_in(key, 23), jnp.arange(NK, dtype=jnp.int32))


def block_levels(own_key, dims, pieces, smallest, largest):
    loudness = 1.0
    for axis_at, blocks in pieces:
        steps = jax.random.uniform(jax.random.fold_in(jax.random.fold_in(own_key, 6), axis_at), (blocks,), jnp.float32, smallest / len(pieces), largest / len(pieces))
        loudness = loudness * jnp.repeat(jnp.exp(steps), dims[axis_at] // blocks).reshape((-1,) + (1,) * (len(dims) - 1 - axis_at))
    return loudness


def gaussian(stream_key, shape, scale, most, pieces=(), kind=jnp.bfloat16):
    result = scale * jax.random.normal(stream_key, shape, jnp.float32)
    if pieces:
        result = result * block_levels(stream_key, shape, pieces, -0.22, 0.18)
    return jnp.clip(result, -most, most).astype(kind)


def setup_inputs(seed: int = 0) -> dict:
    key_of = jax.random.split(jax.random.key(seed), 5)
    return {
        "slab_half": gaussian(key_of[0], (N_REP, NI * BS, KH * BS), 1.0, 6.0, ((0, 2), (1, 8), (2, 16)), jnp.float32),
        "window_half": gaussian(key_of[1], (N_REP, KH * BS, NK * BS), (KL * BS) ** -0.5, 0.125, ((0, 2), (1, 8), (2, 16)), jnp.float32),
        "slab_cols": draw_slab_cols(jax.random.fold_in(key_of[4], 71), 0),
        "window_cols": draw_window_cols(jax.random.fold_in(key_of[4], 71), 0),
    }


def block_mask(columns, width):
    hit = columns[:, :, None] == jnp.arange(width, dtype=jnp.int32)[None, None, :]
    return jnp.any(hit, axis=1)


def expand(mask):
    filled = mask.astype(jnp.float32)
    return jnp.repeat(jnp.repeat(filled, BS, axis=0), BS, axis=1)


def reference(slab_half, window_half, slab_cols, window_cols):
    mask_a = expand(block_mask(slab_cols, NK))
    mask_b = expand(block_mask(window_cols, NK))
    square = jnp.zeros((NI * BS, NK * BS), jnp.float32)
    for half in range(N_REP):
        lower = half * KH * BS
        left = slab_half[half] * mask_a[:, lower:lower + KH * BS]
        right = window_half[half] * mask_b[lower:lower + KH * BS, :]
        square = square + jnp.dot(left, right, precision=lax.Precision.HIGHEST, preferred_element_type=jnp.float32)
    return square * mask_a
```

```python
import jax
import jax.numpy as jnp
from jax import lax
from jax.experimental import pallas as pl
from jax.experimental.pallas import tpu as pltpu
from jax.sharding import PartitionSpec as P

BS = 128
BAND = 24
KL = 20
MESH = pl.DeviceIdType.MESH
G = 4
W = BAND // G
NG = 16
T = G * BS
NX, NY, NZ = 4, 4, 8
NEAR = (0, -1, 1, -2, 2, -3, 3, 4)


def close(a, b):
    return (a - b <= W) & (b - a <= W)


def gather_kernel(slab, window, a_out, b_out, bounce_a, bounce_b, local_sem, za_recv, b_recv, share_recv,
                  z_send, zr_send, y_send, yr_send, x_send, xr_send, c_send, s_send):
    row, col, rep = lax.axis_index("row"), lax.axis_index("col"), lax.axis_index("rep")
    x, core = row // 2, row % 2
    y, zh = col // 4, col % 4
    z = zh * 2 + rep
    mine = 2 * row + rep
    other = 2 * row + 1 - rep

    def at_z(off):
        t = (z + off + NZ) % NZ
        return {"row": row, "col": y * 4 + t // 2, "rep": t % 2}

    def at_y(off):
        return {"row": row, "col": ((y + off + NY) % NY) * 4 + zh, "rep": rep}

    def at_x(off):
        return {"row": ((x + off + NX) % NX) * 2 + core, "col": col, "rep": rep}

    partner = {"row": x * 2 + 1 - core, "col": col, "rep": rep}
    across = {"row": row, "col": col, "rep": 1 - rep}

    barrier = pltpu.get_barrier_semaphore()
    friends = [at_z(1), at_z(-1), at_z(2), at_z(-2), at_y(1), at_y(-1), at_x(1), at_x(-1), partner]
    for f in friends:
        pl.semaphore_signal(barrier, inc=1, device_id=f, device_id_type=MESH)
    pl.semaphore_wait(barrier, len(friends))

    later = []

    def begin(cond, copy):
        @pl.when(cond)
        def _():
            copy.start()

        @later.append
        def _():
            @pl.when(cond)
            def _():
                copy.wait_send()

    def piece_of(off, ys):
        s = (z + off + NZ) % NZ
        q = (s % 2) * 16 + ys * 4 + s // 2
        return q, q // 2

    H = T // 2

    def a_half(q, h):
        return a_out.at[q, pl.ds(h * H, H)]

    def a_copy(src, q, h, send, dest):
        return pltpu.make_async_remote_copy(
            src_ref=src, dst_ref=a_half(q, h), send_sem=send, recv_sem=za_recv.at[q, h],
            device_id=dest, device_id_type=MESH)

    def a_wait(q, h, cond):
        @pl.when(cond)
        def _():
            pltpu.make_async_remote_copy(
                src_ref=a_half(q, h), dst_ref=a_half(q, h), send_sem=za_recv.at[q, h],
                recv_sem=za_recv.at[q, h], device_id=at_z(1), device_id_type=MESH).wait_recv()

    def b_half(k, h):
        return b_out.at[k, pl.ds(h * H, H)]

    def b_copy(src, k, h, send, recv, dest):
        return pltpu.make_async_remote_copy(
            src_ref=src, dst_ref=b_half(k, h), send_sem=send, recv_sem=recv.at[k, h],
            device_id=dest, device_id_type=MESH)

    def b_wait(k, h, cond, recv):
        @pl.when(cond)
        def _():
            pltpu.make_async_remote_copy(
                src_ref=b_half(k, h), dst_ref=b_half(k, h), send_sem=recv.at[k, h],
                recv_sem=recv.at[k, h], device_id=at_z(1), device_id_type=MESH).wait_recv()

    q0, k0 = piece_of(0, y)
    own_in = close(mine, k0)
    opp_in = close(other, k0)

    def own(parity, h):
        return slab.at[0, pl.ds(parity * T + h * H, H)]

    for h in range(2):
        begin(opp_in, a_copy(own(1 - rep, h), q0, h, z_send.at[0, h], at_z(1)))
        begin(opp_in, a_copy(own(1 - rep, h), q0, h, z_send.at[1, h], at_z(-1)))
    for h in range(2):
        begin(own_in, a_copy(own(rep, h), q0, h, z_send.at[2, h], at_z(2)))
        begin(own_in, a_copy(own(rep, 1 - h), q0, 1 - h, z_send.at[3, 1 - h], at_z(-2)))

    kb = rep * 8 + row
    kc = (1 - rep) * 8 + row
    kb_in, kc_in = close(kb, col), close(kc, col)

    def b_first(k, cond, src, n):
        for h in range(2):
            begin(cond, b_copy(src(h), k, h, x_send.at[n, 0, h], b_recv, at_x(1 if h == 0 else -1)))
        for h in range(2):
            begin(cond, b_copy(src(h), k, h, x_send.at[n, 1, h], b_recv, at_x(-1 if h == 0 else 1)))
        for h in range(2):
            begin(cond, b_copy(src(h), k, h, s_send.at[n, h], share_recv, partner))

    def own_b(h):
        return window.at[0, pl.ds(h * H, H)]

    for h in range(2):
        begin(kb_in, b_copy(own_b(h), kb, h, c_send.at[h], b_recv, across))
    b_first(kb, kb_in, own_b, 0)

    in_a = pltpu.make_async_copy(slab.at[0, pl.ds(rep * T, T)], bounce_a, local_sem.at[0])
    in_b = pltpu.make_async_copy(window.at[0], bounce_b, local_sem.at[1])
    in_a.start()
    in_b.start()

    def wants(k, yd):
        c = ((yd + NY) % NY) * 4 + zh
        return close(mine, k) & close(c, k) & close(mine, c)

    def y_first(n):
        q, k = piece_of(NEAR[n], y)
        up, down, far = wants(k, y + 1), wants(k, y - 1), wants(k, y + 2)
        for h in range(2):
            src = own(rep, h) if n == 0 else a_half(q, h)
            begin(up | far if h == 0 else up, a_copy(src, q, h, y_send.at[n, 0, h], at_y(1)))
        for h in (1, 0):
            src = own(rep, h) if n == 0 else a_half(q, h)
            begin(down | far if h == 1 else down, a_copy(src, q, h, y_send.at[n, 1, h], at_y(-1)))

    def y_relay(n):
        here_next = None
        q, k = piece_of(NEAR[n], (y + NY - 1) % NY)
        need, onward = wants(k, y), wants(k, y + 1)
        a_wait(q, 0, need | onward)
        begin(onward, a_copy(a_half(q, 0), q, 0, yr_send.at[n, 0], at_y(1)))
        q2, k2 = piece_of(NEAR[n], (y + 1) % NY)
        need2, onward2 = wants(k2, y), wants(k2, y - 1)
        a_wait(q2, 1, need2 | onward2)
        begin(onward2, a_copy(a_half(q2, 1), q2, 1, yr_send.at[n, 1], at_y(-1)))

    def y_rest(n):
        q, k = piece_of(NEAR[n], (y + NY - 1) % NY)
        a_wait(q, 1, wants(k, y))
        q, k = piece_of(NEAR[n], (y + 1) % NY)
        a_wait(q, 0, wants(k, y))
        q, k = piece_of(NEAR[n], (y + 2) % NY)
        for h in range(2):
            a_wait(q, h, wants(k, y))

    y_first(0)

    for n, d in ((1, -1), (2, 1)):
        q, k = piece_of(d, y)
        c = close(mine, k)
        for h in range(2):
            a_wait(q, h, c)
            begin(c, a_copy(a_half(q, h), q, h, zr_send.at[n - 1, h], at_z(-2 * d)))
        y_first(n)
    y_relay(0)

    for n, d, h in ((3, -2, 0), (4, 2, 1)):
        q, k = piece_of(d, y)
        c = close(mine, k)
        a_wait(q, h, c)
        begin(c, a_copy(a_half(q, h), q, h, zr_send.at[2, h], at_z(-d)))
        a_wait(q, 1 - h, c)
        y_first(n)
    y_relay(1)

    for h in range(2):
        b_wait(kc, h, kc_in, b_recv)
    b_first(kc, kc_in, lambda h: b_half(kc, h), 1)

    def b_from(n, off):
        p = rep if n == 0 else 1 - rep
        k = p * 8 + ((x + off + NX) % NX) * 2 + core
        return k, close(k, col)

    def b_relay(n):
        for off, h in ((-1, 0), (1, 1)):
            k, cond = b_from(n, off)
            b_wait(k, h, cond, b_recv)
            begin(cond, b_copy(b_half(k, h), k, h, xr_send.at[n, h], b_recv, at_x(-off)))
            begin(cond, b_copy(b_half(k, h), k, h, s_send.at[2 + n * 3 + (off + 1) // 2, h], share_recv, partner))

    def b_rest(n):
        for off, h in ((-1, 1), (1, 0)):
            k, cond = b_from(n, off)
            b_wait(k, h, cond, b_recv)
            begin(cond, b_copy(b_half(k, h), k, h, s_send.at[2 + n * 3 + (off + 1) // 2, h], share_recv, partner))
        k, cond = b_from(n, 2)
        for h in range(2):
            b_wait(k, h, cond, b_recv)
            begin(cond, b_copy(b_half(k, h), k, h, s_send.at[2 + n * 3 + 2, h], share_recv, partner))

    b_relay(0)
    y_relay(2)

    for n, d in ((5, -3), (6, 3), (7, 4)):
        q, k = piece_of(d, y)
        for h in range(2):
            a_wait(q, h, close(mine, k))
        y_first(n)
        y_relay(n - 2)
    b_relay(1)
    b_rest(0)
    y_relay(6)
    y_relay(7)
    b_rest(1)

    in_a.wait()
    in_b.wait()
    put_a = pltpu.make_async_copy(bounce_a, a_out.at[q0], local_sem.at[2])
    put_b = pltpu.make_async_copy(bounce_b, b_out.at[kb], local_sem.at[3])
    put_a.start()
    put_b.start()

    for n in range(8):
        y_rest(n)
    for m in range(8):
        k = m * 2 + 1 - core
        for h in range(2):
            b_wait(k, h, close(k, col), share_recv)
    put_a.wait()
    put_b.wait()
    for end in later:
        end()


def gather(slab, window):
    dma = pltpu.SemaphoreType.DMA
    hbm = pl.BlockSpec(memory_space=pl.ANY)
    return pl.pallas_call(
        gather_kernel,
        out_shape=(jax.ShapeDtypeStruct((2 * NG, T, T // 2), jnp.float32),
                   jax.ShapeDtypeStruct((NG, T, T), jnp.float32)),
        in_specs=[hbm, hbm],
        out_specs=(hbm, hbm),
        scratch_shapes=[
            pltpu.VMEM((T, T // 2), jnp.float32), pltpu.VMEM((T, T), jnp.float32),
            dma((4,)), dma((2 * NG, 2)), dma((NG, 2)), dma((NG, 2)),
            dma((4, 2)), dma((3, 2)), dma((8, 2, 2)), dma((8, 2)),
            dma((2, 2, 2)), dma((2, 2)), dma((2,)), dma((8, 2)),
        ],
        compiler_params=pltpu.CompilerParams(collective_id=0, has_side_effects=True),
        name="gather",
    )(slab, window)


def split(v):
    high = v.astype(jnp.bfloat16)
    return high, (v - high.astype(jnp.float32)).astype(jnp.bfloat16)


def product_kernel(span, slab_cols, window_cols, a_ref, b_ref, out_ref):
    s = pl.program_id(0)
    lo, count, rows, cols = span[0], span[1], span[2], span[3]
    lane = lax.broadcasted_iota(jnp.int32, (1, T), 1) // BS

    def listed(table, at, first):
        hit = jnp.zeros((1, T), jnp.float32)
        for t in range(KL):
            hit = jnp.where(lane == table[at, t] - first, 1.0, hit)
        return hit

    @pl.when(s == 0)
    def _():
        out_ref[...] = jnp.zeros_like(out_ref)

    @pl.when(s < count)
    def _():
        k = lo + s
        left, right = [], []
        for i in range(G):
            keep = listed(slab_cols, rows * G + i, k * G)
            part = jnp.concatenate([a_ref[0, 0, i * BS:(i + 1) * BS], a_ref[0, 1, i * BS:(i + 1) * BS]], axis=1)
            left.append(part * keep)
            keep = listed(window_cols, k * G + i, cols * G)
            right.append(b_ref[0, i * BS:(i + 1) * BS] * keep)
        lh, ll = split(jnp.concatenate(left, axis=0))
        rh, rl = split(jnp.concatenate(right, axis=0))
        dot = lambda u, v: jnp.dot(u, v, preferred_element_type=jnp.float32)
        out_ref[...] += dot(lh, rh) + (dot(lh, rl) + dot(ll, rh))

    @pl.when(s == pl.num_programs(0) - 1)
    def _():
        for i in range(G):
            part = slice(i * BS, (i + 1) * BS)
            out_ref[part, :] = out_ref[part, :] * listed(slab_cols, rows * G + i, cols * G)


def multiply(span, slab_cols, window_cols, a, b):
    at = lambda s, span, *_: (span[0] + jnp.minimum(s, jnp.maximum(span[1] - 1, 0)), 0, 0)
    at4 = lambda s, span, *_: (span[0] + jnp.minimum(s, jnp.maximum(span[1] - 1, 0)), 0, 0, 0)
    return pl.pallas_call(
        product_kernel,
        grid_spec=pltpu.PrefetchScalarGridSpec(
            num_scalar_prefetch=3, grid=(2 * W + 1,),
            in_specs=[pl.BlockSpec((1, 2, T, T // 2), at4), pl.BlockSpec((1, T, T), at)],
            out_specs=pl.BlockSpec((T, T), lambda s, *_: (0, 0))),
        out_shape=jax.ShapeDtypeStruct((T, T), jnp.float32),
        compiler_params=pltpu.CompilerParams(dimension_semantics=("arbitrary",)),
        name="multiply",
    )(span, slab_cols, window_cols, a.reshape(NG, 2, T, T // 2), b)


def body(slab_half, window_half, slab_cols, window_cols):
    mine = 2 * lax.axis_index("row") + lax.axis_index("rep")
    col = lax.axis_index("col")
    a, b = gather(slab_half, window_half)
    lo = jnp.maximum(jnp.maximum(mine, col) - W, 0)
    hi = jnp.minimum(jnp.minimum(mine, col) + W, NG - 1)
    count = jnp.where(close(mine, col), jnp.maximum(hi - lo + 1, 0), 0)
    span = jnp.stack([jnp.minimum(lo, NG - 1), count, mine, col]).astype(jnp.int32)
    return multiply(span, slab_cols, window_cols, a, b)


def solution(mesh):
    in_specs = (P("rep", "row", "col"), P("rep", "row", "col"), P(), P())
    out_specs = P(("row", "rep"), "col")
    return jax.shard_map(body, mesh=mesh, in_specs=in_specs, out_specs=out_specs, check_vma=False)
```

```python
import jax
import jax.numpy as jnp
from jax import lax
from jax.experimental import pallas as pl
from jax.experimental.pallas import tpu as pltpu
from jax.sharding import PartitionSpec as P

BS = 128
BAND = 24
KL = 20
MESH = pl.DeviceIdType.MESH
G = 4
W = BAND // G
NG = 16
T = G * BS
NX, NY, NZ, NH = 4, 4, 8, 4
ST = T // NG
HK = KL // 2
HT = T // 2


def close(a, b):
    return (a - b <= W) & (b - a <= W)


def gather_kernel(slab, window, slab_cols, g_out, b_out, strips, packed, bounce, local_sem, e_recv, g_recv, b_recv,
                  share_recv, e_send, z_send, zr_send, y_send, yr_send, x_send, xr_send, c_send, s_send):
    row, col, rep = lax.axis_index("row"), lax.axis_index("col"), lax.axis_index("rep")
    x, core = row // 2, row % 2
    y, zh = col // NH, col % NH
    z = zh * 2 + rep
    mine = 2 * row + rep
    other = 2 * row + 1 - rep

    def at_plane(oy, oz):
        t = (z + oz) % NZ
        return {"row": row, "col": ((y + oy) % NY) * NH + t // 2, "rep": t % 2}

    def at_h(off):
        return {"row": row, "col": y * NH + (zh + off + NH) % NH, "rep": rep}

    def at_y(off):
        return {"row": row, "col": ((y + off + NY) % NY) * NH + zh, "rep": rep}

    def at_x(off):
        return {"row": ((x + off + NX) % NX) * 2 + core, "col": col, "rep": rep}

    partner = {"row": x * 2 + 1 - core, "col": col, "rep": rep}
    across = {"row": row, "col": col, "rep": 1 - rep}
    plane = [(oy, oz) for oz in (4, 3, 5, 2, 6, 1, 7, 0) for oy in (2, 1, 3, 0) if (oy, oz) != (0, 0)]

    barrier = pltpu.get_barrier_semaphore()
    friends = [at_plane(oy, oz) for oy, oz in plane] + [at_x(1), at_x(-1), partner]
    for f in friends:
        pl.semaphore_signal(barrier, inc=1, device_id=f, device_id_type=MESH)
    pl.semaphore_wait(barrier, len(friends))

    later = []

    def begin(cond, copy):
        @pl.when(cond)
        def _():
            copy.start()

        @later.append
        def _():
            @pl.when(cond)
            def _():
                copy.wait_send()

    def send(src, dst, sem, recv, dest):
        return pltpu.make_async_remote_copy(
            src_ref=src, dst_ref=dst, send_sem=sem, recv_sem=recv, device_id=dest, device_id_type=MESH)

    def landed(cond, dst, recv):
        @pl.when(cond)
        def _():
            send(dst, dst, recv, recv, partner).wait_recv()

    q0 = rep * NG + col
    k0 = q0 // 2
    own_in, opp_in = close(mine, k0), close(other, k0)

    def rows_for(p, c):
        return slab.at[0, pl.ds(p * T + c * ST, ST)]

    for n, (oy, oz) in enumerate(plane):
        d = at_plane(oy, oz)
        begin(own_in if oz % 2 == 0 else opp_in,
              send(rows_for(d["rep"], d["col"]), strips.at[q0], e_send.at[n], e_recv.at[q0], d))
    keep_strip = pltpu.make_async_copy(rows_for(rep, col), strips.at[q0], local_sem.at[0])
    keep_strip.start()

    def b_half(k, h):
        return b_out.at[k, pl.ds(h * HT, HT)]

    def own_b(h):
        return window.at[0, pl.ds(h * HT, HT)]

    def wants_b(k, xd):
        first = 4 * ((xd + NX) % NX) + rep
        second = first + 2
        return close(k, col) & ((close(first, col) & close(first, k)) | (close(second, col) & close(second, k)))

    twin = 2 * (x * 2 + 1 - core) + rep

    def b_share(k, h, src, n):
        cond = close(k, col) & close(twin, col) & close(twin, k)
        begin(cond, send(src, b_half(k, h), s_send.at[n, h], share_recv.at[k, h], partner))

    def b_first(k, src, n):
        up, down, far = wants_b(k, x + 1), wants_b(k, x - 1), wants_b(k, x + 2)
        for lead in (0, 1):
            h = lead
            begin(up | far if lead == 0 else up,
                  send(src(h), b_half(k, h), x_send.at[n, 0, h], b_recv.at[k, h], at_x(1)))
            h = 1 - lead
            begin(down | far if lead == 0 else down,
                  send(src(h), b_half(k, h), x_send.at[n, 1, h], b_recv.at[k, h], at_x(-1)))
        for h in range(2):
            b_share(k, h, src(h), n)

    kb = rep * 8 + row
    kc = (1 - rep) * 8 + row
    kb_in, kc_in = close(kb, col), close(kc, col)
    for h in range(2):
        begin(kb_in, send(own_b(h), b_half(kb, h), c_send.at[h], b_recv.at[kb, h], across))
    b_first(kb, own_b, 0)
    take_b = pltpu.make_async_copy(window.at[0], bounce, local_sem.at[1])
    take_b.start()

    def b_from(n, off):
        p = rep if n == 0 else 1 - rep
        return p * 8 + ((x + off + NX) % NX) * 2 + core

    def b_relay(n):
        for off, h in ((-1, 0), (1, 1)):
            k = b_from(n, off)
            onward = wants_b(k, x - off)
            landed(wants_b(k, x) | onward, b_half(k, h), b_recv.at[k, h])
            begin(onward, send(b_half(k, h), b_half(k, h), xr_send.at[n, h], b_recv.at[k, h], at_x(-off)))
            b_share(k, h, b_half(k, h), 2 + n * 3 + (off + 1) // 2)

    def b_rest(n):
        for off, h in ((-1, 1), (1, 0)):
            k = b_from(n, off)
            landed(wants_b(k, x), b_half(k, h), b_recv.at[k, h])
            b_share(k, h, b_half(k, h), 2 + n * 3 + (off + 1) // 2)
        k = b_from(n, 2)
        for h in range(2):
            landed(wants_b(k, x), b_half(k, h), b_recv.at[k, h])
            b_share(k, h, b_half(k, h), 2 + n * 3 + 2)

    take_b.wait()
    put_b = pltpu.make_async_copy(bounce, b_out.at[kb], local_sem.at[2])
    put_b.start()
    b_relay(0)

    keep_strip.wait()
    for oz in range(NZ):
        for oy in range(NY):
            if (oy, oz) == (0, 0):
                continue
            t = (z + oz) % NZ
            q = (t % 2) * NG + ((y + oy) % NY) * NH + t // 2
            landed(close(mine, q // 2), strips.at[q], e_recv.at[q])
    for t in range(KL):
        k = slab_cols[mine * G + y, t]
        both = strips[k // 2]
        packed[t] = jnp.where(k % 2 == 0, both[:, :BS], both[:, BS:])

    def place(i, s, h):
        return g_out.at[i, pl.ds(h * HK, HK), pl.ds(s * ST, ST)]

    def own_g(h):
        return packed.at[pl.ds(h * HK, HK)]

    def g_send(src, i, s, h, sem, dest):
        return send(src, place(i, s, h), sem, g_recv.at[i, s, h], dest)

    always = rep >= 0

    def wants_g(yd):
        return close(mine, ((yd + NY) % NY) * NH + zh)

    here, up, down, far = wants_g(y), wants_g(y + 1), wants_g(y - 1), wants_g(y + 2)

    for lead in range(2):
        begin(always, g_send(own_g(lead), y, zh, lead, z_send.at[0, lead], at_h(1)))
        begin(always, g_send(own_g(1 - lead), y, zh, 1 - lead, z_send.at[1, 1 - lead], at_h(-1)))

    def y_first(n, off):
        s = (zh + off + NH) % NH
        for lead in range(2):
            h = lead
            begin(up | far if lead == 0 else up,
                  g_send(own_g(h) if n == 0 else place(y, s, h), y, s, h, y_send.at[n, 0, h], at_y(1)))
            h = 1 - lead
            begin(down | far if lead == 0 else down,
                  g_send(own_g(h) if n == 0 else place(y, s, h), y, s, h, y_send.at[n, 1, h], at_y(-1)))

    def y_relay(n, off):
        s = (zh + off + NH) % NH
        for d, h in ((-1, 0), (1, 1)):
            i = (y + d + NY) % NY
            onward = wants_g(y - d)
            landed(here | onward, place(i, s, h), g_recv.at[i, s, h])
            begin(onward, g_send(place(i, s, h), i, s, h, yr_send.at[n, h], at_y(-d)))

    def y_rest(n, off):
        s = (zh + off + NH) % NH
        for d, h in ((-1, 1), (1, 0), (2, 0), (2, 1)):
            i = (y + d + NY) % NY
            landed(here, place(i, s, h), g_recv.at[i, s, h])

    y_first(0, 0)
    put_g = pltpu.make_async_copy(packed, g_out.at[y, :, pl.ds(zh * ST, ST)], local_sem.at[3])
    put_g.start()

    for h in range(2):
        landed(kc_in, b_half(kc, h), b_recv.at[kc, h])
    b_first(kc, lambda h: b_half(kc, h), 1)

    for n, off, h in ((1, -1, 0), (2, 1, 1)):
        s = (zh + off + NH) % NH
        landed(always, place(y, s, h), g_recv.at[y, s, h])
        begin(always, g_send(place(y, s, h), y, s, h, zr_send.at[h], at_h(-off)))
    b_rest(0)
    for n, off, h in ((1, -1, 1), (2, 1, 0)):
        s = (zh + off + NH) % NH
        landed(always, place(y, s, h), g_recv.at[y, s, h])
        y_first(n, off)
    y_relay(0, 0)
    s = (zh + 2) % NH
    for h in range(2):
        landed(always, place(y, s, h), g_recv.at[y, s, h])
    y_first(3, 2)
    y_relay(1, -1)
    b_relay(1)
    y_relay(2, 1)
    y_relay(3, 2)
    b_rest(1)

    for n, off in enumerate((0, -1, 1, 2)):
        y_rest(n, off)
    for m in range(8):
        k = m * 2 + 1 - core
        for h in range(2):
            landed(close(k, col) & close(mine, col) & close(mine, k), b_half(k, h), share_recv.at[k, h])
    put_g.wait()
    put_b.wait()
    for end in later:
        end()


def gather(slab, window, slab_cols):
    dma = pltpu.SemaphoreType.DMA
    hbm = pl.BlockSpec(memory_space=pl.ANY)
    return pl.pallas_call(
        gather_kernel,
        out_shape=(jax.ShapeDtypeStruct((G, KL, BS, BS), jnp.float32),
                   jax.ShapeDtypeStruct((NG, T, T), jnp.float32)),
        in_specs=[hbm, hbm, pl.BlockSpec(memory_space=pltpu.SMEM)],
        out_specs=(hbm, hbm),
        scratch_shapes=[
            pltpu.VMEM((2 * NG, ST, 2 * BS), jnp.float32), pltpu.VMEM((KL, ST, BS), jnp.float32),
            pltpu.VMEM((T, T), jnp.float32),
            dma((4,)), dma((2 * NG,)), dma((NY, NH, 2)), dma((NG, 2)), dma((NG, 2)),
            dma((31,)), dma((2, 2)), dma((2,)), dma((4, 2, 2)), dma((4, 2)),
            dma((2, 2, 2)), dma((2, 2)), dma((2,)), dma((8, 2)),
        ],
        compiler_params=pltpu.CompilerParams(collective_id=0, has_side_effects=True),
        name="gather",
    )(slab, window, slab_cols)


def split(v):
    high = v.astype(jnp.bfloat16)
    return high, (v - high.astype(jnp.float32)).astype(jnp.bfloat16)


STEPS = 2 * W + 1


def product_kernel(span, slab_cols, window_cols, g_ref, b_ref, out_ref, b_high, b_low):
    s = pl.program_id(0)
    lo, count, rows, cols = span[0], span[1], span[2], span[3]
    lane = lax.broadcasted_iota(jnp.int32, (1, T), 1) // BS

    def listed(table, at, first):
        hit = jnp.zeros((1, T), jnp.float32)
        for t in range(KL):
            hit = jnp.where(lane == table[at, t] - first, 1.0, hit)
        return hit

    @pl.when(s < count)
    def _():
        for i in range(G):
            keep = listed(window_cols, (lo + s) * G + i, cols * G)
            high, low = split(b_ref[0, i * BS:(i + 1) * BS] * keep)
            b_high[s * G + i] = high
            b_low[s * G + i] = low

    @pl.when((s >= STEPS) & (count == 0))
    def _():
        out_ref[...] = jnp.zeros_like(out_ref)

    @pl.when((s >= STEPS) & (count > 0))
    def _():
        at = rows * G + s - STEPS
        total = jnp.zeros((BS, T), jnp.float32)
        for t in range(0, KL, 2):
            left, high, low = [], [], []
            for u in (t, t + 1):
                k = slab_cols[at, u] - lo * G
                valid = (k >= 0) & (k < count * G)
                k = jnp.where(valid, k, 0)
                left.append(g_ref[0, u] * jnp.where(valid, 1.0, 0.0))
                high.append(b_high[k])
                low.append(b_low[k])
            lh, ll = split(jnp.concatenate(left, axis=1))
            rh, rl = jnp.concatenate(high, axis=0), jnp.concatenate(low, axis=0)
            two = jnp.dot(jnp.concatenate([lh, ll], axis=0), rh, preferred_element_type=jnp.float32)
            total = total + (two[:BS] + (two[BS:] + jnp.dot(lh, rl, preferred_element_type=jnp.float32)))
        out_ref[...] = total * listed(slab_cols, at, cols * G)


def multiply(span, slab_cols, window_cols, g, b):
    at_b = lambda s, span, *_: (span[0] + jnp.minimum(s, jnp.maximum(span[1] - 1, 0)), 0, 0)
    at_g = lambda s, *_: (jnp.maximum(s - STEPS, 0), 0, 0, 0)
    return pl.pallas_call(
        product_kernel,
        grid_spec=pltpu.PrefetchScalarGridSpec(
            num_scalar_prefetch=3, grid=(STEPS + G,),
            in_specs=[pl.BlockSpec((1, KL, BS, BS), at_g), pl.BlockSpec((1, T, T), at_b)],
            out_specs=pl.BlockSpec((BS, T), lambda s, *_: (jnp.maximum(s - STEPS, 0), 0)),
            scratch_shapes=[pltpu.VMEM((STEPS * G, BS, T), jnp.bfloat16)] * 2),
        out_shape=jax.ShapeDtypeStruct((T, T), jnp.float32),
        compiler_params=pltpu.CompilerParams(dimension_semantics=("arbitrary",)),
        name="multiply",
    )(span, slab_cols, window_cols, g, b)


def body(slab_half, window_half, slab_cols, window_cols):
    mine = 2 * lax.axis_index("row") + lax.axis_index("rep")
    col = lax.axis_index("col")
    g, b = gather(slab_half, window_half, slab_cols)
    lo = jnp.maximum(jnp.maximum(mine, col) - W, 0)
    hi = jnp.minimum(jnp.minimum(mine, col) + W, NG - 1)
    count = jnp.where(close(mine, col), jnp.maximum(hi - lo + 1, 0), 0)
    span = jnp.stack([jnp.minimum(lo, NG - 1), count, mine, col]).astype(jnp.int32)
    return multiply(span, slab_cols, window_cols, g, b)


def solution(mesh):
    in_specs = (P("rep", "row", "col"), P("rep", "row", "col"), P(), P())
    out_specs = P(("row", "rep"), "col")
    return jax.shard_map(body, mesh=mesh, in_specs=in_specs, out_specs=out_specs, check_vma=False)
```

```python
import jax
import jax.numpy as jnp
from jax import lax
from jax.experimental import pallas as pl
from jax.experimental.pallas import tpu as pltpu
from jax.sharding import PartitionSpec as P

BS = 128
BAND = 24
KL = 20
MESH = pl.DeviceIdType.MESH
G = 4
W = BAND // G
NG = 16
T = G * BS
NX, NY, NZ, NH = 4, 4, 8, 4
ST = T // NG
HK = KL // 2
HT = T // 2


def close(a, b):
    return (a - b <= W) & (b - a <= W)


def split(v):
    high = v.astype(jnp.bfloat16)
    return high, (v - high.astype(jnp.float32)).astype(jnp.bfloat16)


def listed(table, at, first):
    lane = lax.broadcasted_iota(jnp.int32, (1, T), 1) // BS
    hit = jnp.zeros((1, T), jnp.float32)
    for t in range(KL):
        hit = jnp.where(lane == table[t, at] - first, 1.0, hit)
    return hit


def square_kernel(slab, window, slab_cols, window_cols, out, strips, blocks, tiles, high, low, local_sem, e_recv,
                  g_recv, b_recv, share_recv, e_send, z_send, zr_send, y_send, yr_send, x_send, xr_send, c_send,
                  s_send):
    row, col, rep = lax.axis_index("row"), lax.axis_index("col"), lax.axis_index("rep")
    x, core = row // 2, row % 2
    y, zh = col // NH, col % NH
    z = zh * 2 + rep
    mine = 2 * row + rep
    other = 2 * row + 1 - rep

    def at_plane(oy, oz):
        t = (z + oz) % NZ
        return {"row": row, "col": ((y + oy) % NY) * NH + t // 2, "rep": t % 2}

    def at_h(off):
        return {"row": row, "col": y * NH + (zh + off + NH) % NH, "rep": rep}

    def at_y(off):
        return {"row": row, "col": ((y + off + NY) % NY) * NH + zh, "rep": rep}

    def at_x(off):
        return {"row": ((x + off + NX) % NX) * 2 + core, "col": col, "rep": rep}

    partner = {"row": x * 2 + 1 - core, "col": col, "rep": rep}
    across = {"row": row, "col": col, "rep": 1 - rep}
    plane = [(oy, oz) for oz in (4, 3, 5, 2, 6, 1, 7, 0) for oy in (2, 1, 3, 0) if (oy, oz) != (0, 0)]

    barrier = pltpu.get_barrier_semaphore()
    friends = [at_plane(oy, oz) for oy, oz in plane] + [at_x(1), at_x(-1), partner]
    for f in friends:
        pl.semaphore_signal(barrier, inc=1, device_id=f, device_id_type=MESH)
    pl.semaphore_wait(barrier, len(friends))

    later = []

    def begin(cond, copy):
        @pl.when(cond)
        def _():
            copy.start()

        @later.append
        def _():
            @pl.when(cond)
            def _():
                copy.wait_send()

    def send(src, dst, sem, recv, dest):
        return pltpu.make_async_remote_copy(
            src_ref=src, dst_ref=dst, send_sem=sem, recv_sem=recv, device_id=dest, device_id_type=MESH)

    def landed(cond, dst, recv):
        @pl.when(cond)
        def _():
            send(dst, dst, recv, recv, partner).wait_recv()

    q0 = rep * NG + col
    k0 = q0 // 2
    own_in, opp_in = close(mine, k0), close(other, k0)

    def rows_for(p, c):
        return slab.at[0, pl.ds(p * T + c * ST, ST)]

    for n, (oy, oz) in enumerate(plane):
        d = at_plane(oy, oz)
        begin(own_in if oz % 2 == 0 else opp_in,
              send(rows_for(d["rep"], d["col"]), strips.at[q0], e_send.at[n], e_recv.at[q0], d))
    keep_strip = pltpu.make_async_copy(rows_for(rep, col), strips.at[q0], local_sem.at[0])
    keep_strip.start()

    def b_half(k, h):
        return tiles.at[k, pl.ds(h * HT, HT)]

    def own_b(h):
        return window.at[0, pl.ds(h * HT, HT)]

    def wants_b(k, xd):
        first = 4 * ((xd + NX) % NX) + rep
        second = first + 2
        return close(k, col) & ((close(first, col) & close(first, k)) | (close(second, col) & close(second, k)))

    twin = 2 * (x * 2 + 1 - core) + rep

    def b_share(k, h, src, n):
        cond = close(k, col) & close(twin, col) & close(twin, k)
        begin(cond, send(src, b_half(k, h), s_send.at[n, h], share_recv.at[k, h], partner))

    def b_first(k, src, n):
        up, down, far = wants_b(k, x + 1), wants_b(k, x - 1), wants_b(k, x + 2)
        for lead in (0, 1):
            h = lead
            begin(up | far if lead == 0 else up,
                  send(src(h), b_half(k, h), x_send.at[n, 0, h], b_recv.at[k, h], at_x(1)))
            h = 1 - lead
            begin(down | far if lead == 0 else down,
                  send(src(h), b_half(k, h), x_send.at[n, 1, h], b_recv.at[k, h], at_x(-1)))
        for h in range(2):
            b_share(k, h, src(h), n)

    kb = rep * 8 + row
    kc = (1 - rep) * 8 + row
    kb_in, kc_in = close(kb, col), close(kc, col)
    for h in range(2):
        begin(kb_in, send(own_b(h), b_half(kb, h), c_send.at[h], b_recv.at[kb, h], across))
    b_first(kb, own_b, 0)
    keep_tile = pltpu.make_async_copy(window.at[0], tiles.at[kb], local_sem.at[1])
    keep_tile.start()

    def b_from(n, off):
        p = rep if n == 0 else 1 - rep
        return p * 8 + ((x + off + NX) % NX) * 2 + core

    def b_relay(n):
        for off, h in ((-1, 0), (1, 1)):
            k = b_from(n, off)
            onward = wants_b(k, x - off)
            landed(wants_b(k, x) | onward, b_half(k, h), b_recv.at[k, h])
            begin(onward, send(b_half(k, h), b_half(k, h), xr_send.at[n, h], b_recv.at[k, h], at_x(-off)))
            b_share(k, h, b_half(k, h), 2 + n * 3 + (off + 1) // 2)

    def b_rest(n):
        for off, h in ((-1, 1), (1, 0)):
            k = b_from(n, off)
            landed(wants_b(k, x), b_half(k, h), b_recv.at[k, h])
            b_share(k, h, b_half(k, h), 2 + n * 3 + (off + 1) // 2)
        k = b_from(n, 2)
        for h in range(2):
            landed(wants_b(k, x), b_half(k, h), b_recv.at[k, h])
            b_share(k, h, b_half(k, h), 2 + n * 3 + 2)

    b_relay(0)

    keep_strip.wait()
    for oz in range(NZ):
        for oy in range(NY):
            if (oy, oz) == (0, 0):
                continue
            t = (z + oz) % NZ
            q = (t % 2) * NG + ((y + oy) % NY) * NH + t // 2
            landed(close(mine, q // 2), strips.at[q], e_recv.at[q])
    for t in range(KL):
        k = slab_cols[t, mine * G + y]
        both = strips[k // 2]
        blocks[y, t, pl.ds(zh * ST, ST), :] = jnp.where(k % 2 == 0, both[:, :BS], both[:, BS:])

    def place(i, s, h):
        return blocks.at[i, pl.ds(h * HK, HK), pl.ds(s * ST, ST)]

    def own_g(h):
        return place(y, zh, h)

    def g_send(src, i, s, h, sem, dest):
        return send(src, place(i, s, h), sem, g_recv.at[i, s, h], dest)

    always = rep >= 0

    def wants_g(yd):
        return close(mine, ((yd + NY) % NY) * NH + zh)

    here, up, down, far = wants_g(y), wants_g(y + 1), wants_g(y - 1), wants_g(y + 2)

    for lead in range(2):
        begin(always, g_send(own_g(lead), y, zh, lead, z_send.at[0, lead], at_h(1)))
        begin(always, g_send(own_g(1 - lead), y, zh, 1 - lead, z_send.at[1, 1 - lead], at_h(-1)))

    def y_first(n, off):
        s = (zh + off + NH) % NH
        for lead in range(2):
            h = lead
            begin(up | far if lead == 0 else up,
                  g_send(place(y, s, h), y, s, h, y_send.at[n, 0, h], at_y(1)))
            h = 1 - lead
            begin(down | far if lead == 0 else down,
                  g_send(place(y, s, h), y, s, h, y_send.at[n, 1, h], at_y(-1)))

    def y_relay(n, off):
        s = (zh + off + NH) % NH
        for d, h in ((-1, 0), (1, 1)):
            i = (y + d + NY) % NY
            onward = wants_g(y - d)
            landed(here | onward, place(i, s, h), g_recv.at[i, s, h])
            begin(onward, g_send(place(i, s, h), i, s, h, yr_send.at[n, h], at_y(-d)))

    def y_rest(n, off):
        s = (zh + off + NH) % NH
        for d, h in ((-1, 1), (1, 0), (2, 0), (2, 1)):
            i = (y + d + NY) % NY
            landed(here, place(i, s, h), g_recv.at[i, s, h])

    y_first(0, 0)

    for h in range(2):
        landed(kc_in, b_half(kc, h), b_recv.at[kc, h])
    b_first(kc, lambda h: b_half(kc, h), 1)

    for n, off, h in ((1, -1, 0), (2, 1, 1)):
        s = (zh + off + NH) % NH
        landed(always, place(y, s, h), g_recv.at[y, s, h])
        begin(always, g_send(place(y, s, h), y, s, h, zr_send.at[h], at_h(-off)))
    b_rest(0)
    for n, off, h in ((1, -1, 1), (2, 1, 0)):
        s = (zh + off + NH) % NH
        landed(always, place(y, s, h), g_recv.at[y, s, h])
        y_first(n, off)
    y_relay(0, 0)
    s = (zh + 2) % NH
    for h in range(2):
        landed(always, place(y, s, h), g_recv.at[y, s, h])
    y_first(3, 2)
    y_relay(1, -1)
    b_relay(1)
    y_relay(2, 1)
    y_relay(3, 2)
    b_rest(1)

    for m in range(8):
        k = m * 2 + 1 - core
        for h in range(2):
            landed(close(k, col) & close(mine, col) & close(mine, k), b_half(k, h), share_recv.at[k, h])
    keep_tile.wait()

    active = close(mine, col)
    lo = jnp.maximum(jnp.maximum(mine, col) - W, 0)
    hi = jnp.minimum(jnp.minimum(mine, col) + W, NG - 1)

    @pl.when(active)
    def _():
        @pl.loop(lo, hi + 1)
        def _(k):
            for i in range(G):
                keep = listed(window_cols, k * G + i, col * G)
                h, l = split(tiles[k, i * BS:(i + 1) * BS] * keep)
                high[k * G + i] = h
                low[k * G + i] = l

    for n, off in enumerate((0, -1, 1, 2)):
        y_rest(n, off)

    @pl.when(active)
    def _():
        @pl.loop(0, G)
        def _(r):
            at = mine * G + r
            total = jnp.zeros((BS, T), jnp.float32)
            for t in range(0, KL, 2):
                a, bh, bl = [], [], []
                for u in (t, t + 1):
                    k = slab_cols[u, at]
                    valid = (k >= lo * G) & (k < hi * G + G)
                    k = jnp.where(valid, k, lo * G)
                    a.append(blocks[r, u] * jnp.where(valid, 1.0, 0.0))
                    bh.append(high[k])
                    bl.append(low[k])
                ah, al = split(jnp.concatenate(a, axis=1))
                rh, rl = jnp.concatenate(bh, axis=0), jnp.concatenate(bl, axis=0)
                two = jnp.dot(jnp.concatenate([ah, al], axis=0), rh, preferred_element_type=jnp.float32)
                total = total + (two[:BS] + (two[BS:] + jnp.dot(ah, rl, preferred_element_type=jnp.float32)))
            out[pl.ds(pl.multiple_of(r * BS, BS), BS), :] = total * listed(slab_cols, at, col * G)

    @pl.when(jnp.logical_not(active))
    def _():
        out[...] = jnp.zeros_like(out)

    for end in later:
        end()


def square(slab, window, slab_cols, window_cols):
    dma = pltpu.SemaphoreType.DMA
    hbm = pl.BlockSpec(memory_space=pl.ANY)
    table = pl.BlockSpec(memory_space=pltpu.SMEM)
    return pl.pallas_call(
        square_kernel,
        out_shape=jax.ShapeDtypeStruct((T, T), jnp.float32),
        in_specs=[hbm, hbm, table, table],
        out_specs=pl.BlockSpec(memory_space=pltpu.VMEM),
        scratch_shapes=[
            pltpu.VMEM((2 * NG, ST, 2 * BS), jnp.float32), pltpu.VMEM((G, KL, BS, BS), jnp.float32),
            pltpu.VMEM((NG, T, T), jnp.float32),
            pltpu.VMEM((NG * G, BS, T), jnp.bfloat16), pltpu.VMEM((NG * G, BS, T), jnp.bfloat16),
            dma((2,)), dma((2 * NG,)), dma((NY, NH, 2)), dma((NG, 2)), dma((NG, 2)),
            dma((31,)), dma((2, 2)), dma((2,)), dma((4, 2, 2)), dma((4, 2)),
            dma((2, 2, 2)), dma((2, 2)), dma((2,)), dma((8, 2)),
        ],
        compiler_params=pltpu.CompilerParams(
            collective_id=0, has_side_effects=True, vmem_limit_bytes=60 << 20),
        name="square",
    )(slab, window, slab_cols, window_cols)


def body(slab_half, window_half, slab_cols, window_cols):
    return square(slab_half, window_half, slab_cols.T, window_cols.T)


def solution(mesh):
    in_specs = (P("rep", "row", "col"), P("rep", "row", "col"), P(), P())
    out_specs = P(("row", "rep"), "col")
    return jax.shard_map(body, mesh=mesh, in_specs=in_specs, out_specs=out_specs, check_vma=False)
```

```python
import functools

import jax
import jax.numpy as jnp
from jax import lax
from jax.experimental import pallas as pl
from jax.experimental.pallas import tpu as pltpu
from jax.sharding import PartitionSpec as P

BS = 128
BAND = 24
KL = 20
MESH = pl.DeviceIdType.MESH
G = 4
W = BAND // G
NG = 16
T = G * BS
NX, NY, NZ, NH = 4, 4, 8, 4
ST = T // NG
CUT = (0, 10, KL)
HT = T // 2
ORDER = ("e", "f", "c0", "x", "b000", "b011", "p", "z", "c1", "y00", "y01", "k0", "zp0", "zp1", "b001", "b010", "zl0", "y10", "y11", "zl1", "y20", "y21", "k1", "r0", "bf0", "zf0", "zf1", "y30", "y31", "r1", "b100", "b111", "r2", "r3", "b101", "b110", "bf1")


def close(a, b):
    return (a - b <= W) & (b - a <= W)


def split(v):
    high = v.astype(jnp.bfloat16)
    return high, (v - high.astype(jnp.float32)).astype(jnp.bfloat16)


def listed(table, at, first):
    lane = lax.broadcasted_iota(jnp.int32, (1, T), 1) // BS
    hit = jnp.zeros((1, T), jnp.float32)
    for t in range(KL):
        hit = jnp.where(lane == table[t, at] - first, 1.0, hit)
    return hit


def square_kernel(slab, window, slab_cols, window_cols, out, strips, blocks, tiles, high, low, ready, local_sem, e_recv,
                  g_recv, b_recv, share_recv, e_send, z_send, zr_send, y_send, yr_send, x_send, xr_send, c_send,
                  s_send):
    row, col, rep = lax.axis_index("row"), lax.axis_index("col"), lax.axis_index("rep")
    x, core = row // 2, row % 2
    y, zh = col // NH, col % NH
    z = zh * 2 + rep
    mine = 2 * row + rep
    other = 2 * row + 1 - rep

    def at_plane(oy, oz):
        t = (z + oz) % NZ
        return {"row": row, "col": ((y + oy) % NY) * NH + t // 2, "rep": t % 2}

    def at_h(off):
        return {"row": row, "col": y * NH + (zh + off + NH) % NH, "rep": rep}

    def at_y(off):
        return {"row": row, "col": ((y + off + NY) % NY) * NH + zh, "rep": rep}

    def at_x(off):
        return {"row": ((x + off + NX) % NX) * 2 + core, "col": col, "rep": rep}

    partner = {"row": x * 2 + 1 - core, "col": col, "rep": rep}
    across = {"row": row, "col": col, "rep": 1 - rep}
    plane = [(oy, oz) for oz in (4, 3, 5, 2, 6, 1, 7, 0) for oy in (2, 1, 3, 0) if (oy, oz) != (0, 0)]

    barrier = pltpu.get_barrier_semaphore()
    near = [(oy, oz) for oy, oz in plane if oy == 0 or oz == 0]
    friends = [at_plane(oy, oz) for oy, oz in near] + [at_x(1), at_x(-1), partner]
    for f in friends:
        pl.semaphore_signal(barrier, inc=1, device_id=f, device_id_type=MESH)
    pl.semaphore_wait(barrier, len(friends))
    for oy in range(1, NY):
        pl.semaphore_signal(ready, inc=1, device_id=at_y(oy), device_id_type=MESH)

    later = []

    def begin(cond, copy):
        @pl.when(cond)
        def _():
            copy.start()

        @later.append
        def _():
            @pl.when(cond)
            def _():
                copy.wait_send()

    def send(src, dst, sem, recv, dest):
        return pltpu.make_async_remote_copy(
            src_ref=src, dst_ref=dst, send_sem=sem, recv_sem=recv, device_id=dest, device_id_type=MESH)

    def landed(cond, dst, recv):
        @pl.when(cond)
        def _():
            send(dst, dst, recv, recv, partner).wait_recv()

    q0 = rep * NG + col
    k0 = q0 // 2
    own_in, opp_in = close(mine, k0), close(other, k0)

    def rows_for(p, c):
        return slab.at[0, pl.ds(p * T + c * ST, ST)]

    keep_strip = pltpu.make_async_copy(rows_for(rep, col), strips.at[q0], local_sem.at[0])

    def exchange(close_by):
        if not close_by:
            pl.semaphore_wait(ready, NY - 1)
        for n, (oy, oz) in enumerate(plane):
            if ((oy, oz) in near) != close_by:
                continue
            d = at_plane(oy, oz)
            begin(own_in if oz % 2 == 0 else opp_in,
                  send(rows_for(d["rep"], d["col"]), strips.at[q0], e_send.at[n], e_recv.at[q0], d))
        if close_by:
            keep_strip.start()

    def b_half(k, h):
        return tiles.at[k, pl.ds(h * HT, HT)]

    def own_b(h):
        return window.at[0, pl.ds(h * HT, HT)]

    def wants_b(k, xd):
        first = 4 * ((xd + NX) % NX) + rep
        second = first + 2
        return close(k, col) & ((close(first, col) & close(first, k)) | (close(second, col) & close(second, k)))

    twin = 2 * (x * 2 + 1 - core) + rep

    def b_share(k, h, src, n):
        cond = close(k, col) & close(twin, col) & close(twin, k)
        begin(cond, send(src, b_half(k, h), s_send.at[n, h], share_recv.at[k, h], partner))

    def b_first(k, src, n, h):
        up, down, far = wants_b(k, x + 1), wants_b(k, x - 1), wants_b(k, x + 2)
        far_up, far_down = far_ways(up, down, far, h)
        begin(up | far_up, send(src(h), b_half(k, h), x_send.at[n, 0, h], b_recv.at[k, h], at_x(1)))
        begin(down | far_down, send(src(h), b_half(k, h), x_send.at[n, 1, h], b_recv.at[k, h], at_x(-1)))

    nothing = rep < 0

    def far_ways(up, down, far, h):
        return (far, nothing) if h == 0 else (nothing, far)

    kb = rep * 8 + row
    kc = (1 - rep) * 8 + row
    kb_in, kc_in = close(kb, col), close(kc, col)
    keep_tile = pltpu.make_async_copy(window.at[0], tiles.at[kb], local_sem.at[1])

    def cross(h):
        begin(kb_in, send(own_b(h), b_half(kb, h), c_send.at[h], b_recv.at[kb, h], across))

    def own_tile():
        for h in range(2):
            b_first(kb, own_b, 0, h)
        for h in range(2):
            b_share(kb, h, own_b(h), 0)
        keep_tile.start()

    def crossed(h):
        landed(kc_in, b_half(kc, h), b_recv.at[kc, h])
        b_first(kc, lambda h: b_half(kc, h), 1, h)
        b_share(kc, h, b_half(kc, h), 1)

    def b_from(n, off):
        p = rep if n == 0 else 1 - rep
        return p * 8 + ((x + off + NX) % NX) * 2 + core

    def from_side(n, off, h):
        k = b_from(n, off)
        up, down, far = wants_b(k, x - off + 1), wants_b(k, x - off - 1), wants_b(k, x - off)
        k_up, k_down, k_far = wants_b(k, x + off + 1), wants_b(k, x + off - 1), wants_b(k, x + off + 2)
        far_up, far_down = far_ways(k_up, k_down, k_far, h)
        onward = far_up if off == -1 else far_down
        landed(wants_b(k, x) | onward, b_half(k, h), b_recv.at[k, h])
        begin(onward, send(b_half(k, h), b_half(k, h), xr_send.at[n, (off + 1) // 2, h], b_recv.at[k, h], at_x(-off)))
        b_share(k, h, b_half(k, h), 2 + n * 3 + (off + 1) // 2)

    def from_far(n):
        k = b_from(n, 2)
        for h in range(2):
            landed(wants_b(k, x), b_half(k, h), b_recv.at[k, h])
            b_share(k, h, b_half(k, h), 2 + n * 3 + 2)

    def pack():
        keep_strip.wait()
        for oz in range(NZ):
            for oy in range(NY):
                if (oy, oz) == (0, 0):
                    continue
                t = (z + oz) % NZ
                q = (t % 2) * NG + ((y + oy) % NY) * NH + t // 2
                landed(close(mine, q // 2), strips.at[q], e_recv.at[q])
        for t in range(KL):
            k = slab_cols[t, mine * G + y]
            both = strips[k // 2]
            blocks[y, t, pl.ds(zh * ST, ST), :] = jnp.where(k % 2 == 0, both[:, :BS], both[:, BS:])

    def place(i, s, h):
        return blocks.at[i, pl.ds(CUT[h], CUT[h + 1] - CUT[h]), pl.ds(s * ST, ST)]

    def g_send(i, s, h, sem, dest):
        return send(place(i, s, h), place(i, s, h), sem, g_recv.at[i, s, h], dest)

    always = rep >= 0

    def wants_g(yd):
        return close(mine, ((yd + NY) % NY) * NH + zh)

    here, up, down, far = wants_g(y), wants_g(y + 1), wants_g(y - 1), wants_g(y + 2)

    def z_own():
        for lead in range(2):
            begin(always, g_send(y, zh, lead, z_send.at[0, lead], at_h(1)))
            begin(always, g_send(y, zh, 1 - lead, z_send.at[1, 1 - lead], at_h(-1)))

    def z_pass(n, off, h):
        s = (zh + off + NH) % NH
        landed(always, place(y, s, h), g_recv.at[y, s, h])
        begin(always, g_send(y, s, h, zr_send.at[h], at_h(-off)))

    def z_land(off, h):
        s = (zh + off + NH) % NH
        landed(always, place(y, s, h), g_recv.at[y, s, h])

    def y_first(n, off, h):
        s = (zh + off + NH) % NH
        begin(up | far if h == 0 else up, g_send(y, s, h, y_send.at[n, 0, h], at_y(1)))
        begin(down | far if h == 1 else down, g_send(y, s, h, y_send.at[n, 1, h], at_y(-1)))

    def y_relay(n, off):
        s = (zh + off + NH) % NH
        for d, h in ((-1, 0), (1, 1)):
            i = (y + d + NY) % NY
            onward = wants_g(y - d)
            landed(here | onward, place(i, s, h), g_recv.at[i, s, h])
            begin(onward, g_send(i, s, h, yr_send.at[n, h], at_y(-d)))

    def row_rest(d):
        i = (y + d + NY) % NY
        for off in OFFS:
            t = (zh + off + NH) % NH
            for h in ((), (1,), (0,), (0, 1))[(0, -1, 1, 2).index(d)]:
                landed(here, place(i, t, h), g_recv.at[i, t, h])

    OFFS = (0, -1, 1, 2)
    steps = {"e": functools.partial(exchange, True), "f": functools.partial(exchange, False), "x": own_tile, "p": pack, "z": z_own}
    for h in range(2):
        steps["c%d" % h] = functools.partial(cross, h)
        steps["k%d" % h] = functools.partial(crossed, h)
        steps["zp%d" % h] = functools.partial(z_pass, 1 + h, 2 * h - 1, h)
        steps["zl%d" % h] = functools.partial(z_land, 2 * h - 1, 1 - h)
        steps["zf%d" % h] = functools.partial(z_land, 2, h)
        steps["bf%d" % h] = functools.partial(from_far, h)
        for n in range(4):
            steps["y%d%d" % (n, h)] = functools.partial(y_first, n, OFFS[n], h)
        for n in range(2):
            for w in range(2):
                steps["b%d%d%d" % (n, w, h)] = functools.partial(from_side, n, 2 * w - 1, h)
    for n in range(4):
        steps["r%d" % n] = functools.partial(y_relay, n, OFFS[n])
    for step in ORDER:
        steps[step]()

    for m in range(8):
        k = m * 2 + 1 - core
        for h in range(2):
            landed(close(k, col) & close(mine, col) & close(mine, k), b_half(k, h), share_recv.at[k, h])
    keep_tile.wait()

    active = close(mine, col)
    lo = jnp.maximum(jnp.maximum(mine, col) - W, 0)
    hi = jnp.minimum(jnp.minimum(mine, col) + W, NG - 1)

    @pl.when(active)
    def _():
        @pl.loop(lo, hi + 1)
        def _(k):
            for i in range(G):
                keep = listed(window_cols, k * G + i, col * G)
                h, l = split(tiles[k, i * BS:(i + 1) * BS] * keep)
                high[k * G + i] = h
                low[k * G + i] = l

    def multiply(r):
        at = mine * G + r
        total = jnp.zeros((BS, T), jnp.float32)
        for t in range(0, KL, 2):
            a, bh, bl = [], [], []
            for u in (t, t + 1):
                k = slab_cols[u, at]
                valid = (k >= lo * G) & (k < hi * G + G)
                k = jnp.where(valid, k, lo * G)
                a.append(blocks[r, u] * jnp.where(valid, 1.0, 0.0))
                bh.append(high[k])
                bl.append(low[k])
            ah, al = split(jnp.concatenate(a, axis=1))
            rh, rl = jnp.concatenate(bh, axis=0), jnp.concatenate(bl, axis=0)
            two = jnp.dot(jnp.concatenate([ah, al], axis=0), rh, preferred_element_type=jnp.float32)
            total = total + (two[:BS] + (two[BS:] + jnp.dot(ah, rl, preferred_element_type=jnp.float32)))
        out[pl.ds(pl.multiple_of(r * BS, BS), BS), :] = total * listed(slab_cols, at, col * G)

    for d in (0, -1, 1, 2):
        row_rest(d)

        @pl.when(active)
        def _():
            multiply((y + d + NY) % NY)

    @pl.when(jnp.logical_not(active))
    def _():
        out[...] = jnp.zeros_like(out)

    for end in later:
        end()


def square(slab, window, slab_cols, window_cols):
    dma = pltpu.SemaphoreType.DMA
    hbm = pl.BlockSpec(memory_space=pl.ANY)
    table = pl.BlockSpec(memory_space=pltpu.SMEM)
    return pl.pallas_call(
        square_kernel,
        out_shape=jax.ShapeDtypeStruct((T, T), jnp.float32),
        in_specs=[hbm, hbm, table, table],
        out_specs=pl.BlockSpec(memory_space=pltpu.VMEM),
        scratch_shapes=[
            pltpu.VMEM((2 * NG, ST, 2 * BS), jnp.float32), pltpu.VMEM((G, KL, BS, BS), jnp.float32),
            pltpu.VMEM((NG, T, T), jnp.float32),
            pltpu.VMEM((NG * G, BS, T), jnp.bfloat16), pltpu.VMEM((NG * G, BS, T), jnp.bfloat16),
            pltpu.SemaphoreType.REGULAR, dma((2,)), dma((2 * NG,)), dma((NY, NH, 2)), dma((NG, 2)), dma((NG, 2)),
            dma((31,)), dma((2, 2)), dma((2,)), dma((4, 2, 2)), dma((4, 2)),
            dma((2, 2, 2)), dma((2, 2, 2)), dma((2,)), dma((8, 2)),
        ],
        compiler_params=pltpu.CompilerParams(
            collective_id=0, has_side_effects=True, vmem_limit_bytes=60 << 20),
        name="square",
    )(slab, window, slab_cols, window_cols)


def body(slab_half, window_half, slab_cols, window_cols):
    return square(slab_half, window_half, slab_cols.T, window_cols.T)


def solution(mesh):
    in_specs = (P("rep", "row", "col"), P("rep", "row", "col"), P(), P())
    out_specs = P(("row", "rep"), "col")
    return jax.shard_map(body, mesh=mesh, in_specs=in_specs, out_specs=out_specs, check_vma=False)
```

```python
import functools

import jax
import jax.numpy as jnp
from jax import lax
from jax.experimental import pallas as pl
from jax.experimental.pallas import tpu as pltpu
from jax.sharding import PartitionSpec as P

BS = 128
BAND = 24
KL = 20
MESH = pl.DeviceIdType.MESH
G = 4
W = BAND // G
NG = 16
T = G * BS
NX, NY, NZ, NH = 4, 4, 8, 4
ST = T // NG
SH = ST // 2
HT = T // 2
ORDER = ("e0", "f0", "c0", "x", "e1", "f1", "b000", "b011", "p0", "z0", "y00", "c1", "p1", "z1", "y01", "k0", "zp0", "y10", "zl1", "y20", "k1", "b001", "b010", "zp1", "y21", "zl0", "y11", "r00", "r01", "zf0", "y30", "zf1", "y31", "b100", "b111", "r10", "r11", "bf0", "r20", "r21", "r30", "r31", "b101", "b110", "bf1")


def close(a, b):
    return (a - b <= W) & (b - a <= W)


def split(v):
    high = v.astype(jnp.bfloat16)
    return high, (v - high.astype(jnp.float32)).astype(jnp.bfloat16)


def listed(table, at, first):
    lane = lax.broadcasted_iota(jnp.int32, (1, T), 1) // BS
    hit = jnp.zeros((1, T), jnp.float32)
    for t in range(KL):
        hit = jnp.where(lane == table[t, at] - first, 1.0, hit)
    return hit


def square_kernel(slab, window, slab_cols, window_cols, out, strips_0, strips_1, blocks, tiles, high, low, ready, local_sem, e_recv,
                  g_recv, b_recv, share_recv, e_send, z_send, zr_send, y_send, yr_send, x_send, xr_send, c_send,
                  s_send):
    row, col, rep = lax.axis_index("row"), lax.axis_index("col"), lax.axis_index("rep")
    x, core = row // 2, row % 2
    y, zh = col // NH, col % NH
    z = zh * 2 + rep
    mine = 2 * row + rep
    other = 2 * row + 1 - rep

    def at_plane(oy, oz):
        t = (z + oz) % NZ
        return {"row": row, "col": ((y + oy) % NY) * NH + t // 2, "rep": t % 2}

    def at_h(off):
        return {"row": row, "col": y * NH + (zh + off + NH) % NH, "rep": rep}

    def at_y(off):
        return {"row": row, "col": ((y + off + NY) % NY) * NH + zh, "rep": rep}

    def at_x(off):
        return {"row": ((x + off + NX) % NX) * 2 + core, "col": col, "rep": rep}

    partner = {"row": x * 2 + 1 - core, "col": col, "rep": rep}
    across = {"row": row, "col": col, "rep": 1 - rep}
    plane = [(oy, oz) for oz in (4, 3, 5, 2, 6, 1, 7, 0) for oy in (2, 1, 3, 0) if (oy, oz) != (0, 0)]

    barrier = pltpu.get_barrier_semaphore()
    near = [(oy, oz) for oy, oz in plane if oy == 0 or oz == 0]
    friends = [at_plane(oy, oz) for oy, oz in near] + [at_x(1), at_x(-1), partner]
    for f in friends:
        pl.semaphore_signal(barrier, inc=1, device_id=f, device_id_type=MESH)
    pl.semaphore_wait(barrier, len(friends))
    for oy in range(1, NY):
        pl.semaphore_signal(ready, inc=1, device_id=at_y(oy), device_id_type=MESH)

    later = []

    def begin(cond, copy):
        @pl.when(cond)
        def _():
            copy.start()

        @later.append
        def _():
            @pl.when(cond)
            def _():
                copy.wait_send()

    def send(src, dst, sem, recv, dest):
        return pltpu.make_async_remote_copy(
            src_ref=src, dst_ref=dst, send_sem=sem, recv_sem=recv, device_id=dest, device_id_type=MESH)

    def landed(cond, dst, recv):
        @pl.when(cond)
        def _():
            send(dst, dst, recv, recv, partner).wait_recv()

    q0 = rep * NG + col
    k0 = q0 // 2
    own_in, opp_in = close(mine, k0), close(other, k0)

    def rows_for(p, c, h):
        return slab.at[0, pl.ds(p * T + c * ST + h * SH, SH)]

    strips = (strips_0, strips_1)

    def strip(q, h):
        return strips[h].at[q]

    keep_strip = [pltpu.make_async_copy(rows_for(rep, col, h), strip(q0, h), local_sem.at[h]) for h in range(2)]

    def exchange(close_by, h):
        if not close_by and h == 0:
            pl.semaphore_wait(ready, NY - 1)
        for n, (oy, oz) in enumerate(plane):
            if ((oy, oz) in near) != close_by:
                continue
            d = at_plane(oy, oz)
            begin(own_in if oz % 2 == 0 else opp_in,
                  send(rows_for(d["rep"], d["col"], h), strip(q0, h), e_send.at[n, h], e_recv.at[q0, h], d))
        if close_by:
            keep_strip[h].start()

    def b_half(k, h):
        return tiles.at[k, pl.ds(h * HT, HT)]

    def own_b(h):
        return window.at[0, pl.ds(h * HT, HT)]

    def wants_b(k, xd):
        first = 4 * ((xd + NX) % NX) + rep
        second = first + 2
        return close(k, col) & ((close(first, col) & close(first, k)) | (close(second, col) & close(second, k)))

    twin = 2 * (x * 2 + 1 - core) + rep

    def b_share(k, h, src, n):
        cond = close(k, col) & close(twin, col) & close(twin, k)
        begin(cond, send(src, b_half(k, h), s_send.at[n, h], share_recv.at[k, h], partner))

    def b_first(k, src, n, h):
        up, down, far = wants_b(k, x + 1), wants_b(k, x - 1), wants_b(k, x + 2)
        far_up, far_down = far_ways(up, down, far, h)
        begin(up | far_up, send(src(h), b_half(k, h), x_send.at[n, 0, h], b_recv.at[k, h], at_x(1)))
        begin(down | far_down, send(src(h), b_half(k, h), x_send.at[n, 1, h], b_recv.at[k, h], at_x(-1)))

    nothing = rep < 0

    def far_ways(up, down, far, h):
        return (far, nothing) if h == 0 else (nothing, far)

    kb = rep * 8 + row
    kc = (1 - rep) * 8 + row
    kb_in, kc_in = close(kb, col), close(kc, col)
    keep_tile = pltpu.make_async_copy(window.at[0], tiles.at[kb], local_sem.at[2])

    def cross(h):
        begin(kb_in, send(own_b(h), b_half(kb, h), c_send.at[h], b_recv.at[kb, h], across))

    def own_tile():
        for h in range(2):
            b_first(kb, own_b, 0, h)
        for h in range(2):
            b_share(kb, h, own_b(h), 0)
        keep_tile.start()

    def crossed(h):
        landed(kc_in, b_half(kc, h), b_recv.at[kc, h])
        b_first(kc, lambda h: b_half(kc, h), 1, h)
        b_share(kc, h, b_half(kc, h), 1)

    def b_from(n, off):
        p = rep if n == 0 else 1 - rep
        return p * 8 + ((x + off + NX) % NX) * 2 + core

    def from_side(n, off, h):
        k = b_from(n, off)
        up, down, far = wants_b(k, x - off + 1), wants_b(k, x - off - 1), wants_b(k, x - off)
        k_up, k_down, k_far = wants_b(k, x + off + 1), wants_b(k, x + off - 1), wants_b(k, x + off + 2)
        far_up, far_down = far_ways(k_up, k_down, k_far, h)
        onward = far_up if off == -1 else far_down
        landed(wants_b(k, x) | onward, b_half(k, h), b_recv.at[k, h])
        begin(onward, send(b_half(k, h), b_half(k, h), xr_send.at[n, (off + 1) // 2, h], b_recv.at[k, h], at_x(-off)))
        b_share(k, h, b_half(k, h), 2 + n * 3 + (off + 1) // 2)

    def from_far(n):
        k = b_from(n, 2)
        for h in range(2):
            landed(wants_b(k, x), b_half(k, h), b_recv.at[k, h])
            b_share(k, h, b_half(k, h), 2 + n * 3 + 2)

    def pack(h):
        keep_strip[h].wait()
        for oz in range(NZ):
            for oy in range(NY):
                if (oy, oz) == (0, 0):
                    continue
                t = (z + oz) % NZ
                q = (t % 2) * NG + ((y + oy) % NY) * NH + t // 2
                landed(close(mine, q // 2), strip(q, h), e_recv.at[q, h])
        for t in range(KL):
            k = slab_cols[t, mine * G + y]
            both = strips[h][k // 2]
            blocks[y, t, pl.ds(zh * ST + h * SH, SH), :] = jnp.where(k % 2 == 0, both[:, :BS], both[:, BS:])

    def place(i, s, h):
        return blocks.at[i, :, pl.ds(s * ST + h * SH, SH)]

    def g_send(i, s, h, sem, dest):
        return send(place(i, s, h), place(i, s, h), sem, g_recv.at[i, s, h], dest)

    always = rep >= 0

    def wants_g(yd):
        return close(mine, ((yd + NY) % NY) * NH + zh)

    here, up, down, far = wants_g(y), wants_g(y + 1), wants_g(y - 1), wants_g(y + 2)

    def z_own(h):
        begin(always, g_send(y, zh, h, z_send.at[0, h], at_h(1)))
        begin(always, g_send(y, zh, h, z_send.at[1, h], at_h(-1)))

    def z_pass(n, off, h):
        s = (zh + off + NH) % NH
        landed(always, place(y, s, h), g_recv.at[y, s, h])
        begin(always, g_send(y, s, h, zr_send.at[h], at_h(-off)))

    def z_land(off, h):
        s = (zh + off + NH) % NH
        landed(always, place(y, s, h), g_recv.at[y, s, h])

    def y_first(n, off, h):
        s = (zh + off + NH) % NH
        begin(up | far if h == 0 else up, g_send(y, s, h, y_send.at[n, 0, h], at_y(1)))
        begin(down | far if h == 1 else down, g_send(y, s, h, y_send.at[n, 1, h], at_y(-1)))

    def y_relay(n, off, h):
        s = (zh + off + NH) % NH
        d = 2 * h - 1
        i = (y + d + NY) % NY
        onward = wants_g(y - d)
        landed(here | onward, place(i, s, h), g_recv.at[i, s, h])
        begin(onward, g_send(i, s, h, yr_send.at[n, h], at_y(-d)))

    def row_rest(d):
        i = (y + d + NY) % NY
        for off in OFFS:
            t = (zh + off + NH) % NH
            for h in ((), (1,), (0,), (0, 1))[(0, -1, 1, 2).index(d)]:
                landed(here, place(i, t, h), g_recv.at[i, t, h])

    OFFS = (0, -1, 1, 2)
    steps = {"x": own_tile}
    for h in range(2):
        steps["e%d" % h] = functools.partial(exchange, True, h)
        steps["f%d" % h] = functools.partial(exchange, False, h)
        steps["p%d" % h] = functools.partial(pack, h)
        steps["z%d" % h] = functools.partial(z_own, h)
        steps["c%d" % h] = functools.partial(cross, h)
        steps["k%d" % h] = functools.partial(crossed, h)
        steps["zp%d" % h] = functools.partial(z_pass, 1 + h, 2 * h - 1, h)
        steps["zl%d" % h] = functools.partial(z_land, 2 * h - 1, 1 - h)
        steps["zf%d" % h] = functools.partial(z_land, 2, h)
        steps["bf%d" % h] = functools.partial(from_far, h)
        for n in range(4):
            steps["y%d%d" % (n, h)] = functools.partial(y_first, n, OFFS[n], h)
            steps["r%d%d" % (n, h)] = functools.partial(y_relay, n, OFFS[n], h)
        for n in range(2):
            for w in range(2):
                steps["b%d%d%d" % (n, w, h)] = functools.partial(from_side, n, 2 * w - 1, h)
    for step in ORDER:
        steps[step]()

    for m in range(8):
        k = m * 2 + 1 - core
        for h in range(2):
            landed(close(k, col) & close(mine, col) & close(mine, k), b_half(k, h), share_recv.at[k, h])
    keep_tile.wait()

    active = close(mine, col)
    lo = jnp.maximum(jnp.maximum(mine, col) - W, 0)
    hi = jnp.minimum(jnp.minimum(mine, col) + W, NG - 1)

    @pl.when(active)
    def _():
        @pl.loop(lo, hi + 1)
        def _(k):
            for i in range(G):
                keep = listed(window_cols, k * G + i, col * G)
                h, l = split(tiles[k, i * BS:(i + 1) * BS] * keep)
                high[k * G + i] = h
                low[k * G + i] = l

    def multiply(r):
        at = mine * G + r
        total = jnp.zeros((BS, T), jnp.float32)
        for t in range(0, KL, 2):
            a, bh, bl = [], [], []
            for u in (t, t + 1):
                k = slab_cols[u, at]
                valid = (k >= lo * G) & (k < hi * G + G)
                k = jnp.where(valid, k, lo * G)
                a.append(blocks[r, u] * jnp.where(valid, 1.0, 0.0))
                bh.append(high[k])
                bl.append(low[k])
            ah, al = split(jnp.concatenate(a, axis=1))
            rh, rl = jnp.concatenate(bh, axis=0), jnp.concatenate(bl, axis=0)
            two = jnp.dot(jnp.concatenate([ah, al], axis=0), rh, preferred_element_type=jnp.float32)
            total = total + (two[:BS] + (two[BS:] + jnp.dot(ah, rl, preferred_element_type=jnp.float32)))
        out[pl.ds(pl.multiple_of(r * BS, BS), BS), :] = total * listed(slab_cols, at, col * G)

    for d in (0, -1, 1, 2):
        row_rest(d)

        @pl.when(active)
        def _():
            multiply((y + d + NY) % NY)

    @pl.when(jnp.logical_not(active))
    def _():
        out[...] = jnp.zeros_like(out)

    for end in later:
        end()


def square(slab, window, slab_cols, window_cols):
    dma = pltpu.SemaphoreType.DMA
    hbm = pl.BlockSpec(memory_space=pl.ANY)
    table = pl.BlockSpec(memory_space=pltpu.SMEM)
    return pl.pallas_call(
        square_kernel,
        out_shape=jax.ShapeDtypeStruct((T, T), jnp.float32),
        in_specs=[hbm, hbm, table, table],
        out_specs=pl.BlockSpec(memory_space=pltpu.VMEM),
        scratch_shapes=[
            pltpu.VMEM((2 * NG, SH, 2 * BS), jnp.float32), pltpu.VMEM((2 * NG, SH, 2 * BS), jnp.float32),
            pltpu.VMEM((G, KL, BS, BS), jnp.float32),
            pltpu.VMEM((NG, T, T), jnp.float32),
            pltpu.VMEM((NG * G, BS, T), jnp.bfloat16), pltpu.VMEM((NG * G, BS, T), jnp.bfloat16),
            pltpu.SemaphoreType.REGULAR, dma((3,)), dma((2 * NG, 2)), dma((NY, NH, 2)), dma((NG, 2)), dma((NG, 2)),
            dma((31, 2)), dma((2, 2)), dma((2,)), dma((4, 2, 2)), dma((4, 2)),
            dma((2, 2, 2)), dma((2, 2, 2)), dma((2,)), dma((8, 2)),
        ],
        compiler_params=pltpu.CompilerParams(
            collective_id=0, has_side_effects=True, vmem_limit_bytes=60 << 20),
        name="square",
    )(slab, window, slab_cols, window_cols)


def body(slab_half, window_half, slab_cols, window_cols):
    return square(slab_half, window_half, slab_cols.T, window_cols.T)


def solution(mesh):
    in_specs = (P("rep", "row", "col"), P("rep", "row", "col"), P(), P())
    out_specs = P(("row", "rep"), "col")
    return jax.shard_map(body, mesh=mesh, in_specs=in_specs, out_specs=out_specs, check_vma=False)
```

```python
import functools

import jax
import jax.numpy as jnp
from jax import lax
from jax.experimental import pallas as pl
from jax.experimental.pallas import tpu as pltpu
from jax.sharding import PartitionSpec as P

BS = 128
BAND = 24
KL = 20
MESH = pl.DeviceIdType.MESH
G = 4
W = BAND // G
NG = 16
T = G * BS
NX, NY, NZ, NH = 4, 4, 8, 4
ST = T // NG
SH = ST // 2
HT = T // 2
ORDER = ("c0", "e0", "f0", "x", "e1", "f1", "b000", "b011", "p0", "z0", "y00", "c1", "p1", "z1", "y01", "k0", "zp0", "y10", "zl1", "y20", "k1", "b001", "b010", "zp1", "y21", "zl0", "y11", "r00", "r01", "zf0", "y30", "zf1", "y31", "b100", "b111", "r10", "r11", "bf0", "r20", "r21", "r30", "r31", "b101", "b110", "bf1")


def close(a, b):
    return (a - b <= W) & (b - a <= W)


def within(i, q):
    return (i - 2 * q - 1 <= BAND) & (2 * q - i <= BAND)


def split(v):
    high = v.astype(jnp.bfloat16)
    return high, (v - high.astype(jnp.float32)).astype(jnp.bfloat16)


def listed(table, at, first):
    lane = lax.broadcasted_iota(jnp.int32, (1, T), 1) // BS
    hit = jnp.zeros((1, T), jnp.float32)
    for t in range(KL):
        hit = jnp.where(lane == table[t, at] - first, 1.0, hit)
    return hit


def square_kernel(slab, window, slab_cols, window_cols, out, strips_0, strips_1, blocks, tiles, high, low, ready, local_sem, e_recv,
                  g_recv, b_recv, share_recv, e_send, z_send, zr_send, y_send, yr_send, x_send, xr_send, c_send,
                  s_send):
    row, col, rep = lax.axis_index("row"), lax.axis_index("col"), lax.axis_index("rep")
    x, core = row // 2, row % 2
    y, zh = col // NH, col % NH
    z = zh * 2 + rep
    mine = 2 * row + rep
    other = 2 * row + 1 - rep

    def at_plane(oy, oz):
        t = (z + oz) % NZ
        return {"row": row, "col": ((y + oy) % NY) * NH + t // 2, "rep": t % 2}

    def at_h(off):
        return {"row": row, "col": y * NH + (zh + off + NH) % NH, "rep": rep}

    def at_y(off):
        return {"row": row, "col": ((y + off + NY) % NY) * NH + zh, "rep": rep}

    def at_x(off):
        return {"row": ((x + off + NX) % NX) * 2 + core, "col": col, "rep": rep}

    partner = {"row": x * 2 + 1 - core, "col": col, "rep": rep}
    across = {"row": row, "col": col, "rep": 1 - rep}
    plane = [(oy, oz) for oz in (4, 3, 5, 2, 6, 1, 7, 0) for oy in (2, 1, 3, 0) if (oy, oz) != (0, 0)]

    barrier = pltpu.get_barrier_semaphore()
    near = [(oy, oz) for oy, oz in plane if oy == 0 or oz == 0]
    friends = [at_plane(oy, oz) for oy, oz in near] + [at_x(1), at_x(-1), partner]
    for f in friends:
        pl.semaphore_signal(barrier, inc=1, device_id=f, device_id_type=MESH)
    pl.semaphore_wait(barrier, len(friends))
    for oy in range(1, NY):
        pl.semaphore_signal(ready, inc=1, device_id=at_y(oy), device_id_type=MESH)

    later = []

    def begin(cond, copy):
        @pl.when(cond)
        def _():
            copy.start()

        @later.append
        def _():
            @pl.when(cond)
            def _():
                copy.wait_send()

    def send(src, dst, sem, recv, dest):
        return pltpu.make_async_remote_copy(
            src_ref=src, dst_ref=dst, send_sem=sem, recv_sem=recv, device_id=dest, device_id_type=MESH)

    def landed(cond, dst, recv):
        @pl.when(cond)
        def _():
            send(dst, dst, recv, recv, partner).wait_recv()

    q0 = rep * NG + col

    def rows_for(p, c, h):
        return slab.at[0, pl.ds(p * T + c * ST + h * SH, SH)]

    strips = (strips_0, strips_1)

    def strip(q, h):
        return strips[h].at[q]

    keep_strip = [pltpu.make_async_copy(rows_for(rep, col, h), strip(q0, h), local_sem.at[h]) for h in range(2)]

    def exchange(close_by, h):
        if not close_by and h == 0:
            pl.semaphore_wait(ready, NY - 1)
        for n, (oy, oz) in enumerate(plane):
            if ((oy, oz) in near) != close_by:
                continue
            d = at_plane(oy, oz)
            target = mine if oz % 2 == 0 else other
            begin(within(target * G + (y + oy) % NY, q0),
                  send(rows_for(d["rep"], d["col"], h), strip(q0, h), e_send.at[n, h], e_recv.at[q0, h], d))
        if close_by:
            keep_strip[h].start()

    def b_half(k, h):
        return tiles.at[k, pl.ds(h * HT, HT)]

    def own_b(h):
        return window.at[0, pl.ds(h * HT, HT)]

    def wants_b(k, xd):
        first = 4 * ((xd + NX) % NX) + rep
        second = first + 2
        return close(k, col) & ((close(first, col) & close(first, k)) | (close(second, col) & close(second, k)))

    twin = 2 * (x * 2 + 1 - core) + rep

    def b_share(k, h, src, n):
        cond = close(k, col) & close(twin, col) & close(twin, k)
        begin(cond, send(src, b_half(k, h), s_send.at[n, h], share_recv.at[k, h], partner))

    def b_first(k, src, n, h):
        up, down, far = wants_b(k, x + 1), wants_b(k, x - 1), wants_b(k, x + 2)
        far_up, far_down = far_ways(up, down, far, h)
        begin(up | far_up, send(src(h), b_half(k, h), x_send.at[n, 0, h], b_recv.at[k, h], at_x(1)))
        begin(down | far_down, send(src(h), b_half(k, h), x_send.at[n, 1, h], b_recv.at[k, h], at_x(-1)))

    nothing = rep < 0

    def far_ways(up, down, far, h):
        return (far, nothing) if h == 0 else (nothing, far)

    kb = rep * 8 + row
    kc = (1 - rep) * 8 + row
    kb_in, kc_in = close(kb, col), close(kc, col)
    keep_tile = pltpu.make_async_copy(window.at[0], tiles.at[kb], local_sem.at[2])

    def cross(h):
        begin(kb_in, send(own_b(h), b_half(kb, h), c_send.at[h], b_recv.at[kb, h], across))

    def own_tile():
        for h in range(2):
            b_first(kb, own_b, 0, h)
        for h in range(2):
            b_share(kb, h, own_b(h), 0)
        keep_tile.start()

    def crossed(h):
        landed(kc_in, b_half(kc, h), b_recv.at[kc, h])
        b_first(kc, lambda h: b_half(kc, h), 1, h)
        b_share(kc, h, b_half(kc, h), 1)

    def b_from(n, off):
        p = rep if n == 0 else 1 - rep
        return p * 8 + ((x + off + NX) % NX) * 2 + core

    def from_side(n, off, h):
        k = b_from(n, off)
        up, down, far = wants_b(k, x - off + 1), wants_b(k, x - off - 1), wants_b(k, x - off)
        k_up, k_down, k_far = wants_b(k, x + off + 1), wants_b(k, x + off - 1), wants_b(k, x + off + 2)
        far_up, far_down = far_ways(k_up, k_down, k_far, h)
        onward = far_up if off == -1 else far_down
        landed(wants_b(k, x) | onward, b_half(k, h), b_recv.at[k, h])
        begin(onward, send(b_half(k, h), b_half(k, h), xr_send.at[n, (off + 1) // 2, h], b_recv.at[k, h], at_x(-off)))
        b_share(k, h, b_half(k, h), 2 + n * 3 + (off + 1) // 2)

    def from_far(n):
        k = b_from(n, 2)
        for h in range(2):
            landed(wants_b(k, x), b_half(k, h), b_recv.at[k, h])
            b_share(k, h, b_half(k, h), 2 + n * 3 + 2)

    def pack(h):
        keep_strip[h].wait()
        for oz in range(NZ):
            for oy in range(NY):
                if (oy, oz) == (0, 0):
                    continue
                t = (z + oz) % NZ
                q = (t % 2) * NG + ((y + oy) % NY) * NH + t // 2
                landed(within(mine * G + y, q), strip(q, h), e_recv.at[q, h])
        for t in range(KL):
            k = slab_cols[t, mine * G + y]
            both = strips[h][k // 2]
            blocks[y, t, pl.ds(zh * ST + h * SH, SH), :] = jnp.where(k % 2 == 0, both[:, :BS], both[:, BS:])

    def place(i, s, h):
        return blocks.at[i, :, pl.ds(s * ST + h * SH, SH)]

    def g_send(i, s, h, sem, dest):
        return send(place(i, s, h), place(i, s, h), sem, g_recv.at[i, s, h], dest)

    always = rep >= 0

    def wants_g(yd):
        return close(mine, ((yd + NY) % NY) * NH + zh)

    here, up, down, far = wants_g(y), wants_g(y + 1), wants_g(y - 1), wants_g(y + 2)

    def z_own(h):
        begin(always, g_send(y, zh, h, z_send.at[0, h], at_h(1)))
        begin(always, g_send(y, zh, h, z_send.at[1, h], at_h(-1)))

    def z_pass(n, off, h):
        s = (zh + off + NH) % NH
        landed(always, place(y, s, h), g_recv.at[y, s, h])
        begin(always, g_send(y, s, h, zr_send.at[h], at_h(-off)))

    def z_land(off, h):
        s = (zh + off + NH) % NH
        landed(always, place(y, s, h), g_recv.at[y, s, h])

    def y_first(n, off, h):
        s = (zh + off + NH) % NH
        begin(up | far if h == 0 else up, g_send(y, s, h, y_send.at[n, 0, h], at_y(1)))
        begin(down | far if h == 1 else down, g_send(y, s, h, y_send.at[n, 1, h], at_y(-1)))

    def y_relay(n, off, h):
        s = (zh + off + NH) % NH
        d = 2 * h - 1
        i = (y + d + NY) % NY
        onward = wants_g(y - d)
        landed(here | onward, place(i, s, h), g_recv.at[i, s, h])
        begin(onward, g_send(i, s, h, yr_send.at[n, h], at_y(-d)))

    def row_rest(d):
        i = (y + d + NY) % NY
        for off in OFFS:
            t = (zh + off + NH) % NH
            for h in ((), (1,), (0,), (0, 1))[(0, -1, 1, 2).index(d)]:
                landed(here, place(i, t, h), g_recv.at[i, t, h])

    OFFS = (0, -1, 1, 2)
    steps = {"x": own_tile}
    for h in range(2):
        steps["e%d" % h] = functools.partial(exchange, True, h)
        steps["f%d" % h] = functools.partial(exchange, False, h)
        steps["p%d" % h] = functools.partial(pack, h)
        steps["z%d" % h] = functools.partial(z_own, h)
        steps["c%d" % h] = functools.partial(cross, h)
        steps["k%d" % h] = functools.partial(crossed, h)
        steps["zp%d" % h] = functools.partial(z_pass, 1 + h, 2 * h - 1, h)
        steps["zl%d" % h] = functools.partial(z_land, 2 * h - 1, 1 - h)
        steps["zf%d" % h] = functools.partial(z_land, 2, h)
        steps["bf%d" % h] = functools.partial(from_far, h)
        for n in range(4):
            steps["y%d%d" % (n, h)] = functools.partial(y_first, n, OFFS[n], h)
            steps["r%d%d" % (n, h)] = functools.partial(y_relay, n, OFFS[n], h)
        for n in range(2):
            for w in range(2):
                steps["b%d%d%d" % (n, w, h)] = functools.partial(from_side, n, 2 * w - 1, h)
    for step in ORDER:
        steps[step]()

    for m in range(8):
        k = m * 2 + 1 - core
        for h in range(2):
            landed(close(k, col) & close(mine, col) & close(mine, k), b_half(k, h), share_recv.at[k, h])
    keep_tile.wait()

    active = close(mine, col)
    lo = jnp.maximum(jnp.maximum(mine, col) - W, 0)
    hi = jnp.minimum(jnp.minimum(mine, col) + W, NG - 1)

    @pl.when(active)
    def _():
        @pl.loop(lo, hi + 1)
        def _(k):
            for i in range(G):
                keep = listed(window_cols, k * G + i, col * G)
                h, l = split(tiles[k, i * BS:(i + 1) * BS] * keep)
                high[k * G + i] = h
                low[k * G + i] = l

    def multiply(r):
        at = mine * G + r
        total = jnp.zeros((BS, T), jnp.float32)
        for t in range(0, KL, 2):
            a, bh, bl = [], [], []
            for u in (t, t + 1):
                k = slab_cols[u, at]
                valid = (k >= lo * G) & (k < hi * G + G)
                k = jnp.where(valid, k, lo * G)
                a.append(blocks[r, u] * jnp.where(valid, 1.0, 0.0))
                bh.append(high[k])
                bl.append(low[k])
            ah, al = split(jnp.concatenate(a, axis=1))
            rh, rl = jnp.concatenate(bh, axis=0), jnp.concatenate(bl, axis=0)
            two = jnp.dot(jnp.concatenate([ah, al], axis=0), rh, preferred_element_type=jnp.float32)
            total = total + (two[:BS] + (two[BS:] + jnp.dot(ah, rl, preferred_element_type=jnp.float32)))
        out[pl.ds(pl.multiple_of(r * BS, BS), BS), :] = total * listed(slab_cols, at, col * G)

    for d in (0, -1, 1, 2):
        row_rest(d)

        @pl.when(active)
        def _():
            multiply((y + d + NY) % NY)

    @pl.when(jnp.logical_not(active))
    def _():
        out[...] = jnp.zeros_like(out)

    for end in later:
        end()


def square(slab, window, slab_cols, window_cols):
    dma = pltpu.SemaphoreType.DMA
    hbm = pl.BlockSpec(memory_space=pl.ANY)
    table = pl.BlockSpec(memory_space=pltpu.SMEM)
    return pl.pallas_call(
        square_kernel,
        out_shape=jax.ShapeDtypeStruct((T, T), jnp.float32),
        in_specs=[hbm, hbm, table, table],
        out_specs=pl.BlockSpec(memory_space=pltpu.VMEM),
        scratch_shapes=[
            pltpu.VMEM((2 * NG, SH, 2 * BS), jnp.float32), pltpu.VMEM((2 * NG, SH, 2 * BS), jnp.float32),
            pltpu.VMEM((G, KL, BS, BS), jnp.float32),
            pltpu.VMEM((NG, T, T), jnp.float32),
            pltpu.VMEM((NG * G, BS, T), jnp.bfloat16), pltpu.VMEM((NG * G, BS, T), jnp.bfloat16),
            pltpu.SemaphoreType.REGULAR, dma((3,)), dma((2 * NG, 2)), dma((NY, NH, 2)), dma((NG, 2)), dma((NG, 2)),
            dma((31, 2)), dma((2, 2)), dma((2,)), dma((4, 2, 2)), dma((4, 2)),
            dma((2, 2, 2)), dma((2, 2, 2)), dma((2,)), dma((8, 2)),
        ],
        compiler_params=pltpu.CompilerParams(
            collective_id=0, has_side_effects=True, vmem_limit_bytes=60 << 20),
        name="square",
    )(slab, window, slab_cols, window_cols)


def body(slab_half, window_half, slab_cols, window_cols):
    return square(slab_half, window_half, slab_cols.T, window_cols.T)


def solution(mesh):
    in_specs = (P("rep", "row", "col"), P("rep", "row", "col"), P(), P())
    out_specs = P(("row", "rep"), "col")
    return jax.shard_map(body, mesh=mesh, in_specs=in_specs, out_specs=out_specs, check_vma=False)
```

```python
import functools

import jax
import jax.numpy as jnp
from jax import lax
from jax.experimental import pallas as pl
from jax.experimental.pallas import tpu as pltpu
from jax.sharding import PartitionSpec as P

BS = 128
BAND = 24
KL = 20
MESH = pl.DeviceIdType.MESH
G = 4
W = BAND // G
NG = 16
T = G * BS
NX, NY, NZ, NH = 4, 4, 8, 4
ST = T // NG
SH = ST // 2
HT = T // 2
ORDER = ("c0", "e0", "f0", "x", "e1", "f1", "b000", "b011", "p0", "z0", "y00", "c1", "p1", "z1", "y01", "k0", "zp0", "y10", "zl1", "y20", "k1", "b001", "b010", "zp1", "y21", "zl0", "y11", "r00", "r01", "zf0", "y30", "zf1", "y31", "b100", "b111", "r10", "r11", "bf0", "r20", "r21", "r30", "r31", "b101", "b110", "bf1")


def close(a, b):
    return (a - b <= W) & (b - a <= W)


def within(i, q):
    return (i - 2 * q - 1 <= BAND) & (2 * q - i <= BAND)


def split(v):
    high = v.astype(jnp.bfloat16)
    return high, (v - high.astype(jnp.float32)).astype(jnp.bfloat16)


def listed(table, at, first):
    lane = lax.broadcasted_iota(jnp.int32, (1, T), 1) // BS
    hit = jnp.zeros((1, T), jnp.float32)
    for t in range(KL):
        hit = jnp.where(lane == table[t, at] - first, 1.0, hit)
    return hit


def square_kernel(slab, window, slab_cols, window_cols, out, strips_0, strips_1, blocks, tiles, high, low, ready, local_sem, e_recv,
                  g_recv, b_recv, share_recv, e_send, z_send, zr_send, y_send, yr_send, x_send, xr_send, c_send,
                  s_send):
    row, col, rep = lax.axis_index("row"), lax.axis_index("col"), lax.axis_index("rep")
    x, core = row // 2, row % 2
    y, zh = col // NH, col % NH
    z = zh * 2 + rep
    mine = 2 * row + rep
    other = 2 * row + 1 - rep

    def at_plane(oy, oz):
        t = (z + oz) % NZ
        return {"row": row, "col": ((y + oy) % NY) * NH + t // 2, "rep": t % 2}

    def at_h(off):
        return {"row": row, "col": y * NH + (zh + off + NH) % NH, "rep": rep}

    def at_y(off):
        return {"row": row, "col": ((y + off + NY) % NY) * NH + zh, "rep": rep}

    def at_x(off):
        return {"row": ((x + off + NX) % NX) * 2 + core, "col": col, "rep": rep}

    partner = {"row": x * 2 + 1 - core, "col": col, "rep": rep}
    across = {"row": row, "col": col, "rep": 1 - rep}
    plane = [(oy, oz) for oz in (4, 3, 5, 2, 6, 1, 7, 0) for oy in (2, 1, 3, 0) if (oy, oz) != (0, 0)]

    barrier = pltpu.get_barrier_semaphore()
    near = [(oy, oz) for oy, oz in plane if oy == 0 or oz == 0]
    friends = [at_plane(oy, oz) for oy, oz in near] + [at_x(1), at_x(-1), partner]
    for f in friends:
        pl.semaphore_signal(barrier, inc=1, device_id=f, device_id_type=MESH)
    pl.semaphore_wait(barrier, len(friends))
    for oy in range(1, NY):
        pl.semaphore_signal(ready, inc=1, device_id=at_y(oy), device_id_type=MESH)

    later = []

    def begin(cond, copy):
        @pl.when(cond)
        def _():
            copy.start()

        @later.append
        def _():
            @pl.when(cond)
            def _():
                copy.wait_send()

    def send(src, dst, sem, recv, dest):
        return pltpu.make_async_remote_copy(
            src_ref=src, dst_ref=dst, send_sem=sem, recv_sem=recv, device_id=dest, device_id_type=MESH)

    def landed(cond, dst, recv):
        @pl.when(cond)
        def _():
            send(dst, dst, recv, recv, partner).wait_recv()

    q0 = rep * NG + col

    def rows_for(p, c, h):
        return slab.at[0, pl.ds(p * T + c * ST + h * SH, SH)]

    strips = (strips_0, strips_1)

    def strip(q, h):
        return strips[h].at[q]

    keep_strip = [pltpu.make_async_copy(rows_for(rep, col, h), strip(q0, h), local_sem.at[h]) for h in range(2)]

    def exchange(close_by, h):
        if not close_by and h == 0:
            pl.semaphore_wait(ready, NY - 1)
        for n, (oy, oz) in enumerate(plane):
            if ((oy, oz) in near) != close_by:
                continue
            d = at_plane(oy, oz)
            target = mine if oz % 2 == 0 else other
            begin(within(target * G + (y + oy) % NY, q0),
                  send(rows_for(d["rep"], d["col"], h), strip(q0, h), e_send.at[n, h], e_recv.at[q0, h], d))
        if close_by:
            keep_strip[h].start()

    def b_half(k, h):
        return tiles.at[k, pl.ds(h * HT, HT)]

    def own_b(h):
        return window.at[0, pl.ds(h * HT, HT)]

    def wants_b(k, xd):
        first = 4 * ((xd + NX) % NX) + rep
        second = first + 2
        return close(k, col) & ((close(first, col) & close(first, k)) | (close(second, col) & close(second, k)))

    twin = 2 * (x * 2 + 1 - core) + rep

    def b_share(k, h, src, n):
        cond = close(k, col) & close(twin, col) & close(twin, k)
        begin(cond, send(src, b_half(k, h), s_send.at[n, h], share_recv.at[k, h], partner))

    def b_first(k, src, n, h, ways=(0, 1)):
        up, down, far = wants_b(k, x + 1), wants_b(k, x - 1), wants_b(k, x + 2)
        far_up, far_down = far_ways(up, down, far, h)
        for w in ways:
            begin((up | far_up, down | far_down)[w],
                  send(src(h), b_half(k, h), x_send.at[n, w, h], b_recv.at[k, h], at_x(1 - 2 * w)))

    nothing = rep < 0

    def far_ways(up, down, far, h):
        return (far, nothing) if h == 0 else (nothing, far)

    kb = rep * 8 + row
    kc = (1 - rep) * 8 + row
    kb_in, kc_in = close(kb, col), close(kc, col)
    keep_tile = pltpu.make_async_copy(window.at[0], tiles.at[kb], local_sem.at[2])

    def cross(h):
        begin(kb_in, send(own_b(h), b_half(kb, h), c_send.at[h], b_recv.at[kb, h], across))

    def own_tile():
        for lead in range(2):
            b_first(kb, own_b, 0, lead, (0,))
            b_first(kb, own_b, 0, 1 - lead, (1,))
        for h in range(2):
            b_share(kb, h, own_b(h), 0)
        keep_tile.start()

    def crossed(h):
        landed(kc_in, b_half(kc, h), b_recv.at[kc, h])
        b_first(kc, lambda h: b_half(kc, h), 1, h)
        b_share(kc, h, b_half(kc, h), 1)

    def b_from(n, off):
        p = rep if n == 0 else 1 - rep
        return p * 8 + ((x + off + NX) % NX) * 2 + core

    def from_side(n, off, h):
        k = b_from(n, off)
        up, down, far = wants_b(k, x - off + 1), wants_b(k, x - off - 1), wants_b(k, x - off)
        k_up, k_down, k_far = wants_b(k, x + off + 1), wants_b(k, x + off - 1), wants_b(k, x + off + 2)
        far_up, far_down = far_ways(k_up, k_down, k_far, h)
        onward = far_up if off == -1 else far_down
        landed(wants_b(k, x) | onward, b_half(k, h), b_recv.at[k, h])
        begin(onward, send(b_half(k, h), b_half(k, h), xr_send.at[n, (off + 1) // 2, h], b_recv.at[k, h], at_x(-off)))
        b_share(k, h, b_half(k, h), 2 + n * 3 + (off + 1) // 2)

    def from_far(n):
        k = b_from(n, 2)
        for h in range(2):
            landed(wants_b(k, x), b_half(k, h), b_recv.at[k, h])
            b_share(k, h, b_half(k, h), 2 + n * 3 + 2)

    def pack(h):
        keep_strip[h].wait()
        for oz in range(NZ):
            for oy in range(NY):
                if (oy, oz) == (0, 0):
                    continue
                t = (z + oz) % NZ
                q = (t % 2) * NG + ((y + oy) % NY) * NH + t // 2
                landed(within(mine * G + y, q), strip(q, h), e_recv.at[q, h])
        for t in range(KL):
            k = slab_cols[t, mine * G + y]
            both = strips[h][k // 2]
            blocks[y, t, pl.ds(zh * ST + h * SH, SH), :] = jnp.where(k % 2 == 0, both[:, :BS], both[:, BS:])

    def place(i, s, h):
        return blocks.at[i, :, pl.ds(s * ST + h * SH, SH)]

    def g_send(i, s, h, sem, dest):
        return send(place(i, s, h), place(i, s, h), sem, g_recv.at[i, s, h], dest)

    always = rep >= 0

    def wants_g(yd):
        return close(mine, ((yd + NY) % NY) * NH + zh)

    here, up, down, far = wants_g(y), wants_g(y + 1), wants_g(y - 1), wants_g(y + 2)

    def z_own(h):
        begin(always, g_send(y, zh, h, z_send.at[0, h], at_h(1)))
        begin(always, g_send(y, zh, h, z_send.at[1, h], at_h(-1)))

    def z_pass(n, off, h):
        s = (zh + off + NH) % NH
        landed(always, place(y, s, h), g_recv.at[y, s, h])
        begin(always, g_send(y, s, h, zr_send.at[h], at_h(-off)))

    def z_land(off, h):
        s = (zh + off + NH) % NH
        landed(always, place(y, s, h), g_recv.at[y, s, h])

    def y_first(n, off, h):
        s = (zh + off + NH) % NH
        begin(up | far if h == 0 else up, g_send(y, s, h, y_send.at[n, 0, h], at_y(1)))
        begin(down | far if h == 1 else down, g_send(y, s, h, y_send.at[n, 1, h], at_y(-1)))

    def y_relay(n, off, h):
        s = (zh + off + NH) % NH
        d = 2 * h - 1
        i = (y + d + NY) % NY
        onward = wants_g(y - d)
        landed(here | onward, place(i, s, h), g_recv.at[i, s, h])
        begin(onward, g_send(i, s, h, yr_send.at[n, h], at_y(-d)))

    def row_rest(d):
        i = (y + d + NY) % NY
        for off in OFFS:
            t = (zh + off + NH) % NH
            for h in ((), (1,), (0,), (0, 1))[(0, -1, 1, 2).index(d)]:
                landed(here, place(i, t, h), g_recv.at[i, t, h])

    OFFS = (0, -1, 1, 2)
    steps = {"x": own_tile}
    for h in range(2):
        steps["e%d" % h] = functools.partial(exchange, True, h)
        steps["f%d" % h] = functools.partial(exchange, False, h)
        steps["p%d" % h] = functools.partial(pack, h)
        steps["z%d" % h] = functools.partial(z_own, h)
        steps["c%d" % h] = functools.partial(cross, h)
        steps["k%d" % h] = functools.partial(crossed, h)
        steps["zp%d" % h] = functools.partial(z_pass, 1 + h, 2 * h - 1, h)
        steps["zl%d" % h] = functools.partial(z_land, 2 * h - 1, 1 - h)
        steps["zf%d" % h] = functools.partial(z_land, 2, h)
        steps["bf%d" % h] = functools.partial(from_far, h)
        for n in range(4):
            steps["y%d%d" % (n, h)] = functools.partial(y_first, n, OFFS[n], h)
            steps["r%d%d" % (n, h)] = functools.partial(y_relay, n, OFFS[n], h)
        for n in range(2):
            for w in range(2):
                steps["b%d%d%d" % (n, w, h)] = functools.partial(from_side, n, 2 * w - 1, h)
    for step in ORDER:
        steps[step]()

    for m in range(8):
        k = m * 2 + 1 - core
        for h in range(2):
            landed(close(k, col) & close(mine, col) & close(mine, k), b_half(k, h), share_recv.at[k, h])
    keep_tile.wait()

    active = close(mine, col)
    lo = jnp.maximum(jnp.maximum(mine, col) - W, 0)
    hi = jnp.minimum(jnp.minimum(mine, col) + W, NG - 1)

    @pl.when(active)
    def _():
        @pl.loop(lo, hi + 1)
        def _(k):
            for i in range(G):
                keep = listed(window_cols, k * G + i, col * G)
                h, l = split(tiles[k, i * BS:(i + 1) * BS] * keep)
                high[k * G + i] = h
                low[k * G + i] = l

    def multiply(r):
        at = mine * G + r
        total = jnp.zeros((BS, T), jnp.float32)
        for t in range(0, KL, 2):
            a, bh, bl = [], [], []
            for u in (t, t + 1):
                k = slab_cols[u, at]
                valid = (k >= lo * G) & (k < hi * G + G)
                k = jnp.where(valid, k, lo * G)
                a.append(blocks[r, u] * jnp.where(valid, 1.0, 0.0))
                bh.append(high[k])
                bl.append(low[k])
            ah, al = split(jnp.concatenate(a, axis=1))
            rh, rl = jnp.concatenate(bh, axis=0), jnp.concatenate(bl, axis=0)
            two = jnp.dot(jnp.concatenate([ah, al], axis=0), rh, preferred_element_type=jnp.float32)
            total = total + (two[:BS] + (two[BS:] + jnp.dot(ah, rl, preferred_element_type=jnp.float32)))
        out[pl.ds(pl.multiple_of(r * BS, BS), BS), :] = total * listed(slab_cols, at, col * G)

    for d in (0, -1, 1, 2):
        row_rest(d)

        @pl.when(active)
        def _():
            multiply((y + d + NY) % NY)

    @pl.when(jnp.logical_not(active))
    def _():
        out[...] = jnp.zeros_like(out)

    for end in later:
        end()


def square(slab, window, slab_cols, window_cols):
    dma = pltpu.SemaphoreType.DMA
    hbm = pl.BlockSpec(memory_space=pl.ANY)
    table = pl.BlockSpec(memory_space=pltpu.SMEM)
    return pl.pallas_call(
        square_kernel,
        out_shape=jax.ShapeDtypeStruct((T, T), jnp.float32),
        in_specs=[hbm, hbm, table, table],
        out_specs=pl.BlockSpec(memory_space=pltpu.VMEM),
        scratch_shapes=[
            pltpu.VMEM((2 * NG, SH, 2 * BS), jnp.float32), pltpu.VMEM((2 * NG, SH, 2 * BS), jnp.float32),
            pltpu.VMEM((G, KL, BS, BS), jnp.float32),
            pltpu.VMEM((NG, T, T), jnp.float32),
            pltpu.VMEM((NG * G, BS, T), jnp.bfloat16), pltpu.VMEM((NG * G, BS, T), jnp.bfloat16),
            pltpu.SemaphoreType.REGULAR, dma((3,)), dma((2 * NG, 2)), dma((NY, NH, 2)), dma((NG, 2)), dma((NG, 2)),
            dma((31, 2)), dma((2, 2)), dma((2,)), dma((4, 2, 2)), dma((4, 2)),
            dma((2, 2, 2)), dma((2, 2, 2)), dma((2,)), dma((8, 2)),
        ],
        compiler_params=pltpu.CompilerParams(
            collective_id=0, has_side_effects=True, vmem_limit_bytes=60 << 20),
        name="square",
    )(slab, window, slab_cols, window_cols)


def body(slab_half, window_half, slab_cols, window_cols):
    return square(slab_half, window_half, slab_cols.T, window_cols.T)


def solution(mesh):
    in_specs = (P("rep", "row", "col"), P("rep", "row", "col"), P(), P())
    out_specs = P(("row", "rep"), "col")
    return jax.shard_map(body, mesh=mesh, in_specs=in_specs, out_specs=out_specs, check_vma=False)
```
